256 devices in a mesh: blk: 64 (over x, z, core), rep: 4 (over y).
Axes of the slice: x: 4, y: 4, z: 8, core: 2. Of those that a mesh axis runs over, the one named last changes fastest.
Arguments:
- query_embed: bfloat16 [64, 4, 256, 256], P('blk', 'rep'), may hold values from -96 to 96
- positive_ids: int32 [64, 4, 256], P('blk'), may hold values from 0 to 16383, as said below
- pair_blocks: int32 [64, 64], P('blk'), may hold values from 0 to 255, as said below
- code_ids: int32 [64, 4, 8, 64], P('blk', 'rep'), may hold values from 0 to 255
- codebooks: bfloat16 [2048, 256], replicated, may hold values from -3 to 3
Outputs:
- query_loss: float32 [64, 4, 256], P('blk', 'rep')
- query_grad: float32 [64, 4, 256, 256], P('blk', 'rep')
- passage_grad: float32 [64, 4, 64, 256], P('blk', 'rep')
- codebook_grad: float32 [2048, 256], P(('blk', 'rep'))
The draws below stay inside these ranges and needn't reach their ends.
Inputs may be any that keep to these rules, and one draw needn't show every extreme that they name: `pair_blocks`: each row names 64 different passage blocks; at most 2 of them belong to one owner o (blocks o * 4 to o * 4 + 3), and in every row some owner has exactly 2. Some blocks are named in many rows. `positive_ids`: the positive passage of a query lies in a block named in its query block's row of pair_blocks.
All inputs are finite; a program needn't handle non-finite values.
Results may differ from the reference program's by a relative error of at most 0.0079.
Values may be sent and summed in bfloat16 or wider, within the bound.
No kernel may reach another device: no remote copies, remote signals or barrier semaphores. Data moves between devices by JAX's collectives and lax.ppermute only.
A program may use at most 64 MiB of HBM per device.

```python
import jax
import jax.numpy as jnp
from jax import lax

E = 256
BOOKS = 8
CODES = 256
QR = 256
PR = 16
PBLK_DEV = 4
CAP = 2
N_BLK = 64
N_REP = 4


def pair_table(key):
    base = jax.random.fold_in(key, 7001)
    first, second, third = jax.random.split(base, 3)
    partition_overall_sum = PBLK_DEV * N_BLK
    extreme_value_perturbation = jax.random.randint(first, (N_BLK, partition_overall_sum), 0, 1 << 20)
    discretization_tier = jax.random.randint(second, (partition_overall_sum,), 0, 4) * (1 << 18)
    shift = jax.random.randint(third, (), 0, N_BLK)
    holding_accelerator = jnp.arange(partition_overall_sum, dtype=jnp.int32) // PBLK_DEV
    imposed_selection = (jnp.arange(N_BLK, dtype=jnp.int32) * 5 + shift) % N_BLK
    hinge_offset = (holding_accelerator[None, :] == imposed_selection[:, None]).astype(jnp.int32) * (1 << 30)
    similarity_logit = (extreme_value_perturbation + discretization_tier[None, :]) * partition_overall_sum + jnp.arange(partition_overall_sum, dtype=jnp.int32)[None, :] + hinge_offset
    grouped = similarity_logit.reshape(N_BLK, N_BLK, PBLK_DEV)
    best, where_at = lax.top_k(grouped, CAP)
    block_ids = jnp.arange(N_BLK, dtype=jnp.int32)[None, :, None] * PBLK_DEV + where_at
    flat_best = best.reshape(N_BLK, N_BLK * CAP)
    flat_ids = block_ids.reshape(N_BLK, N_BLK * CAP)
    unused, picked = lax.top_k(flat_best, N_BLK)
    return jnp.take_along_axis(flat_ids, picked, axis=1).astype(jnp.int32)


def positive_table(key, pairs_drawn):
    base = jax.random.fold_in(key, 7002)
    first, second = jax.random.split(base)
    slot_pick = jax.random.randint(first, (N_BLK, N_REP * QR), 0, N_BLK)
    row_pick = jax.random.randint(second, (N_BLK, N_REP * QR), 0, PR * N_REP)
    chosen = jnp.take_along_axis(pairs_drawn, slot_pick, axis=1)
    return (chosen * (PR * N_REP) + row_pick).reshape(N_BLK, N_REP, QR).astype(jnp.int32)


def code_table(key):
    return jax.random.randint(jax.random.fold_in(key, 7003), (N_BLK, N_REP, BOOKS, PBLK_DEV * PR), 0, CODES).astype(jnp.int32)


def book_table(key):
    values = jax.random.normal(jax.random.fold_in(key, 7004), (BOOKS * CODES, E), jnp.float32) * 0.5
    return jnp.clip(values, -3.0, 3.0).astype(jnp.bfloat16)


def draw_pair_blocks(key, part):
    return pair_table(key)


def draw_positive_ids(key, part):
    return positive_table(key, pair_table(key))


def draw_code_ids(key, part):
    return code_table(key)


def draw_codebooks(key, part):
    return book_table(key)


def draw_query_embed(key, part):
    base = jax.random.fold_in(key, 7005)
    first = jax.random.fold_in(base, 0)
    values = jnp.clip(jax.random.normal(first, (N_BLK, N_REP, QR, E), jnp.float32) * 2.0, -12.0, 12.0)
    return values.astype(jnp.bfloat16)


def setup_inputs(seed: int = 0) -> dict:
    seeds = jax.random.split(jax.random.key(seed), 6)
    return {
        "query_embed": draw_query_embed(jax.random.fold_in(seeds[5], 71), 0),
        "positive_ids": draw_positive_ids(jax.random.fold_in(seeds[5], 71), 0),
        "pair_blocks": draw_pair_blocks(jax.random.fold_in(seeds[5], 71), 0),
        "code_ids": draw_code_ids(jax.random.fold_in(seeds[5], 71), 0),
        "codebooks": draw_codebooks(jax.random.fold_in(seeds[5], 71), 0),
    }


EPS = 1e-06

def reference(query_embed, positive_ids, pair_blocks, code_ids, codebooks):
    block_count, rep_count, query_rows, feat_count = query_embed.shape
    block_rows = PR * rep_count
    pair_count = pair_blocks.shape[1]
    table = codebooks.astype(jnp.float32)
    quant = jnp.zeros((block_count, rep_count, PBLK_DEV * PR, feat_count), jnp.float32)
    for book_index in range(BOOKS):
        quant = quant + table[code_ids[:, :, book_index, :] + book_index * CODES]
    inverse = lax.rsqrt(lax.optimization_barrier(jnp.sum(quant * quant, axis=-1, keepdims=True)) + EPS)
    unit = quant * inverse
    unit_bf = unit.astype(jnp.bfloat16)
    blocks = unit_bf.reshape(block_count, rep_count, PBLK_DEV, PR, feat_count)
    blocks = blocks.transpose(0, 2, 1, 3, 4).reshape(block_count * PBLK_DEV, block_rows, feat_count)
    column_ids = jnp.arange(pair_count * block_rows, dtype=jnp.int32)
    slot_ids = jnp.arange(pair_count, dtype=jnp.int32)

    def one_block(carry, item):
        row_block, targets, chosen = item
        columns = blocks[chosen].reshape(pair_count * block_rows, feat_count)
        scores = jnp.dot(row_block, columns.T, preferred_element_type=jnp.float32)
        peak = lax.optimization_barrier(jnp.max(scores, axis=1, keepdims=True))
        lse = peak[:, 0] + jnp.log(lax.optimization_barrier(jnp.sum(jnp.exp(scores - peak), axis=1)))
        target_block = targets // block_rows
        target_slot = lax.optimization_barrier(jnp.sum(jnp.where(chosen[None, :] == target_block[:, None], slot_ids[None, :], 0), axis=1)).astype(jnp.int32)
        target_col = target_slot * block_rows + targets % block_rows
        hit_mask = column_ids[None, :] == target_col[:, None]
        target = lax.optimization_barrier(jnp.sum(jnp.where(hit_mask, scores, 0.0), axis=1))
        weight = (jnp.exp(scores - lse[:, None]) - hit_mask.astype(jnp.float32)).astype(jnp.bfloat16)
        grad_rows = jnp.dot(weight, columns, preferred_element_type=jnp.float32)
        grad_cols = jnp.dot(weight.T, row_block, preferred_element_type=jnp.float32)
        carry = carry.at[chosen].add(grad_cols.reshape(pair_count, block_rows, feat_count))
        return (carry, (lse - target, grad_rows))
    start = jnp.zeros((block_count * PBLK_DEV, block_rows, feat_count), jnp.float32)
    inputs = (query_embed.reshape(block_count, rep_count * query_rows, feat_count), positive_ids.reshape(block_count, rep_count * query_rows), pair_blocks)
    unit_grad, (losses, grads) = lax.scan(one_block, start, inputs)
    unit_grad = unit_grad.reshape(block_count, PBLK_DEV, rep_count, PR, feat_count)
    unit_grad = unit_grad.transpose(0, 2, 1, 3, 4).reshape(block_count, rep_count, PBLK_DEV * PR, feat_count)
    passage_grad = inverse * (unit_grad - unit * lax.optimization_barrier(jnp.sum(unit * unit_grad, axis=-1, keepdims=True)))
    flat_grad = passage_grad.reshape(-1, feat_count)
    pieces = []
    for book_index in range(BOOKS):
        members = code_ids[:, :, book_index, :].reshape(-1)
        pieces.append(jax.ops.segment_sum(flat_grad, members, num_segments=CODES))
    codebook_grad = jnp.concatenate(pieces, axis=0)
    query_loss = losses.reshape(block_count, rep_count, query_rows)
    query_grad = grads.reshape(block_count, rep_count, query_rows, feat_count)
    return (query_loss, query_grad, passage_grad, codebook_grad)
```

```python
import jax
import jax.numpy as jnp
from jax import lax
from jax.experimental import pallas as pl
from jax.experimental.pallas import tpu as pltpu
from jax.sharding import Mesh
from jax.sharding import PartitionSpec as P


CODES = 256
BOOKS = 8
PR = 16
PBLK_DEV = 4
CAP = 2
LANES = 128
AXES = ("x", "z", "c", "rep")
BLK = ("x", "z", "c")
EPS = 1e-06
INTERPRET = False
VMEM_LIMIT = 24 << 20

F32 = jnp.float32
BF16 = jnp.bfloat16
VMEM = pl.BlockSpec(memory_space=pltpu.VMEM)
SMEM = pl.BlockSpec(memory_space=pltpu.SMEM)
CONTRACT_LAST = (((1,), (1,)), ((), ()))
CONTRACT_FIRST = (((0,), (0,)), ((), ()))


def call(kernel, out_shape, scratch, smem_count, vmem_count, flops):
    out_bytes = sum(s.size * s.dtype.itemsize for s in jax.tree.leaves(out_shape))
    return pl.pallas_call(
        kernel,
        out_shape=out_shape,
        in_specs=[SMEM] * smem_count + [VMEM] * vmem_count,
        out_specs=jax.tree.map(lambda _: VMEM, out_shape),
        scratch_shapes=scratch,
        interpret=INTERPRET,
        compiler_params=pltpu.CompilerParams(vmem_limit_bytes=VMEM_LIMIT),
        cost_estimate=pl.CostEstimate(
            flops=flops, bytes_accessed=2 * out_bytes, transcendentals=0
        ),
    )


def sds(shape, dtype):
    return jax.ShapeDtypeStruct(shape, dtype)


def one_hot_of(codes_ref, book, rows):
    cols = codes_ref.shape[1]
    row = codes_ref[book : book + 1, :]
    iota = lax.broadcasted_iota(jnp.int32, (rows, cols), 0).astype(F32)
    return jnp.where(row == iota, 1.0, 0.0).astype(BF16)


def fill_keys(pair_s, key_ref, pair_count):
    sub = lax.broadcasted_iota(jnp.int32, (PR, LANES), 0)
    for slot in range(pair_count):
        key_ref[slot * PR : (slot + 1) * PR, :] = sub + pair_s[slot] * PR


def hits(key_ref, start, count, tkey_ref):
    keys = key_ref[start : start + count, :]
    width = tkey_ref.shape[1]
    wide = jnp.concatenate([keys] * (width // LANES), axis=1)
    return wide == tkey_ref[...]


def stats_kernel(
    pair_s, place_s, recv_ref, q0, q1, q2, q3, tkey_ref, cbt_ref,
    u_ref, q_ref, st_ref, codes_ref, rows_ref, key_ref,
):
    cols = u_ref.shape[0]
    pair_count = cols // PR
    rep = place_s[3]
    rows = q0.shape[0]
    parts = (q0, q1, q2, q3)
    for k in range(len(parts)):
        owner = lax.rem(rep + len(parts) - k, len(parts))
        q_ref[pl.ds(pl.multiple_of(owner * rows, rows), rows), :] = parts[k][...]
    rows_ref[...] = recv_ref[...].astype(F32)
    lane_group = lax.broadcasted_iota(jnp.int32, (BOOKS, LANES), 1) // PR
    per_tile = LANES // PR
    for tile in range(cols // LANES):
        held = jnp.zeros((BOOKS, LANES), F32)
        for place in range(per_tile):
            block = pair_s[tile * per_tile + place]
            owner = block >> 2
            within = block & 3
            codes = rows_ref[pl.ds(pl.multiple_of(owner * BOOKS, BOOKS), BOOKS), :]
            turned = pltpu.roll(codes, lax.rem(LANES + (place - within) * PR, LANES), axis=1)
            held = jnp.where(lane_group == place, turned, held)
        codes_ref[:, tile * LANES : (tile + 1) * LANES] = held
    fill_keys(pair_s, key_ref, pair_count)
    quant = jnp.zeros((cbt_ref.shape[0], cols), F32)
    for book in range(BOOKS):
        quant = quant + jnp.dot(
            cbt_ref[:, book * CODES : (book + 1) * CODES],
            one_hot_of(codes_ref, book, CODES),
            preferred_element_type=F32,
        )
    inverse = lax.rsqrt(jnp.sum(quant * quant, axis=0, keepdims=True) + EPS)
    u_ref[...] = (quant * inverse).T.astype(BF16)
    total_rows = q_ref.shape[0]
    peak = jnp.full((1, total_rows), -1e30, F32)
    total = jnp.zeros((1, total_rows), F32)
    hit = jnp.zeros((1, total_rows), F32)
    step = min(256, cols)
    for start in range(0, cols, step):
        scores = lax.dot_general(
            u_ref[start : start + step, :], q_ref[...], CONTRACT_LAST, preferred_element_type=F32
        )
        fresh = jnp.maximum(peak, jnp.max(scores, axis=0, keepdims=True))
        total = total * jnp.exp(peak - fresh) + jnp.sum(
            jnp.exp(scores - fresh), axis=0, keepdims=True
        )
        peak = fresh
        hit = hit + jnp.sum(
            jnp.where(hits(key_ref, start, step, tkey_ref), scores, 0.0), axis=0, keepdims=True
        )
    st_ref[0:1, :] = peak
    st_ref[1:2, :] = total
    st_ref[2:3, :] = hit
    st_ref[3:8, :] = jnp.zeros((5, total_rows), F32)


def merged(first, second):
    peak = jnp.maximum(first[0:1], second[0:1])
    total = first[1:2] * jnp.exp(first[0:1] - peak) + second[1:2] * jnp.exp(second[0:1] - peak)
    return peak, total, first[2:3] + second[2:3]


def grads_kernel(
    pair_s, slot_s, place_s, sta_ref, stb_ref, tkey_ref, u_ref, q_ref,
    send_ref, g_ref, loss_ref, own_ref, far1, far2, far3, key_ref, lse_ref, qgt_ref,
):
    cols = u_ref.shape[0]
    pair_count = cols // PR
    rep = place_s[3]
    rows = own_ref.shape[1]
    peak, total, hit = merged(sta_ref[...], stb_ref[...])
    lse = peak + jnp.log(total)
    lse_ref[0:1, :] = lse - hit
    loss_ref[...] = lse_ref[0:1, pl.ds(pl.multiple_of(rep * rows, rows), rows)]
    fill_keys(pair_s, key_ref, pair_count)
    send_ref[...] = jnp.zeros(send_ref.shape, BF16)
    step = min(256, cols)
    grown = None
    for start in range(0, cols, step):
        u_part = u_ref[start : start + step, :]
        scores = lax.dot_general(u_part, q_ref[...], CONTRACT_LAST, preferred_element_type=F32)
        hit_mask = hits(key_ref, start, step, tkey_ref)
        weight = (jnp.exp(scores - lse) - jnp.where(hit_mask, 1.0, 0.0)).astype(BF16)
        grad = jnp.dot(weight, q_ref[...], preferred_element_type=F32)
        g_ref[start : start + step, :] = grad
        narrow = grad.astype(BF16)
        for place in range(step // PR):
            send_ref[slot_s[start // PR + place]] = narrow[place * PR : (place + 1) * PR, :]
        term = lax.dot_general(u_part, weight, CONTRACT_FIRST, preferred_element_type=F32)
        grown = term if grown is None else grown + term
    qgt_ref[...] = grown
    count = q_ref.shape[0] // rows
    for k, out in enumerate((own_ref, far1, far2, far3)):
        owner = lax.rem(rep + k, count)
        part = qgt_ref[:, pl.ds(pl.multiple_of(owner * rows, rows), rows)]
        out[...] = part.astype(out.dtype)


def books_kernel(place_s, codes_ref, cbt_ref, g_ref, keep_ref, send_ref, hot_ref, sum_ref):
    cols = codes_ref.shape[1]
    core = place_s[2]
    quant = jnp.zeros((cbt_ref.shape[0], cols), F32)
    for book in range(BOOKS):
        hot_ref[book] = one_hot_of(codes_ref, book, CODES)
        quant = quant + jnp.dot(
            cbt_ref[:, book * CODES : (book + 1) * CODES],
            hot_ref[book],
            preferred_element_type=F32,
        )
    inverse = lax.rsqrt(jnp.sum(quant * quant, axis=0, keepdims=True) + EPS)
    unit = quant * inverse
    grad = g_ref[...].T
    grad = inverse * (grad - unit * jnp.sum(unit * grad, axis=0, keepdims=True))
    narrow = grad.astype(BF16)
    for book in range(BOOKS):
        sum_ref[book * CODES : (book + 1) * CODES, :] = lax.dot_general(
            hot_ref[book], narrow, CONTRACT_LAST, preferred_element_type=F32
        )
    half = keep_ref.shape[1]
    for chunk in range(keep_ref.shape[0]):
        base = chunk * 2 * half
        keep_ref[chunk] = sum_ref[pl.ds(pl.multiple_of(base + core * half, half), half), :]
        send_ref[chunk] = sum_ref[
            pl.ds(pl.multiple_of(base + (1 - core) * half, half), half), :
        ].astype(BF16)


def x_order(here, count):
    if count == 4:
        return (here, 3 - here, here ^ 1, 3 - (here ^ 1))
    return tuple(here ^ k for k in range(count))


def deal_kernel(place_s, keep_ref, recv_ref, own_ref, far1, far2, far3, sum_ref):
    x_here, z_here, rep = place_s[0], place_s[1], place_s[3]
    x_count, z_count, reps = place_sizes(own_ref, keep_ref)
    share = keep_ref.shape[1] // reps
    sum_ref[...] = keep_ref[...] + recv_ref[...].astype(F32)
    order = x_order(x_here, x_count)
    for k, out in enumerate((own_ref, far1, far2, far3)):
        owner = lax.rem(rep + k, reps)
        at = pl.ds(pl.multiple_of(owner * share, share), share)
        for px in range(x_count):
            for pz in range(z_count):
                chunk = order[px] * z_count + (z_here ^ pz)
                out[px * z_count + pz] = sum_ref[chunk, at, :].astype(out.dtype)


def place_sizes(own_ref, keep_ref):
    chunks = keep_ref.shape[0]
    x_count = 4
    return x_count, chunks // x_count, keep_ref.shape[1] // own_ref.shape[1]


def return_kernel(slot_j, ret_ref, unit_ref, inv_ref, out_ref, *sums):
    for part in sums:
        part[...] = jnp.zeros(part.shape, F32)
    for slot in range(ret_ref.shape[0]):
        part = sums[slot % len(sums)]
        j = slot_j[slot]
        part[j] = part[j] + ret_ref[slot].astype(F32)
    for j in range(PBLK_DEV):
        grad = sums[0][j]
        for part in sums[1:]:
            grad = grad + part[j]
        unit = unit_ref[j * PR : (j + 1) * PR, :]
        inverse = inv_ref[j * PR : (j + 1) * PR, 0:1]
        out_ref[j * PR : (j + 1) * PR, :] = inverse * (
            grad - unit * jnp.sum(unit * grad, axis=1, keepdims=True)
        )


def unit_rows(local_codes, codebooks):
    iota = jnp.arange(CODES, dtype=jnp.int32)
    pieces = [
        (local_codes[book][:, None] == iota[None, :]).astype(BF16)
        for book in range(local_codes.shape[0])
    ]
    quant = jnp.dot(jnp.concatenate(pieces, axis=1), codebooks, preferred_element_type=F32)
    inverse = lax.rsqrt(jnp.sum(quant * quant, axis=1, keepdims=True) + EPS)
    return (quant * inverse, inverse)


def shifted(x, k):
    count = lax.axis_size("rep")
    return lax.ppermute(x, "rep", [(i, (i + k) % count) for i in range(count)])


def halved(own, axis, partner):
    half = own.shape[0] // 2
    pairs = [(i, partner(i)) for i in range(lax.axis_size(axis))]
    arrived = lax.ppermute(own[half:].astype(BF16), axis, pairs)
    return own[:half] + arrived.astype(F32)


def shards(query_embed, positive_ids, pair_blocks, code_ids, codebooks):
    reps = lax.axis_size("rep")
    x_count, z_count, cores = (lax.axis_size(a) for a in BLK)
    owners = x_count * z_count * cores
    here_blk = lax.axis_index(BLK)
    here_rep = lax.axis_index("rep")
    rows_mine = query_embed[0, 0]
    row_count, feat = rows_mine.shape
    all_rows = reps * row_count
    wanted = pair_blocks[0]
    pair_count = wanted.shape[0]
    cols = pair_count * PR
    local_codes = code_ids[0, 0]
    place = jnp.stack([lax.axis_index(a) for a in AXES]).astype(jnp.int32)

    held = local_codes.shape[1]
    listed = jnp.broadcast_to(
        jnp.pad(wanted, (0, LANES - held - pair_count))[None, :], (BOOKS, LANES - held)
    )
    message = jnp.concatenate([local_codes, listed], axis=1).astype(BF16)
    message = jnp.broadcast_to(message[None], (owners, BOOKS, LANES))
    arrived = lax.all_to_all(message, BLK, 0, 0, tiled=True)
    query_parts = [rows_mine] + [shifted(rows_mine, k) for k in range(1, reps)]

    targets = positive_ids[0].reshape(1, all_rows)
    row_in = targets % (PR * reps)
    tkey = jnp.where(
        row_in // PR == here_rep, (targets // (PR * reps)) * PR + row_in % PR, -1
    ).astype(jnp.int32)
    owner_of = wanted // PBLK_DEV
    before_me = jnp.sum(
        ((owner_of[None, :] == owner_of[:, None]) & (wanted[None, :] < wanted[:, None])).astype(
            jnp.int32
        ),
        axis=1,
    )
    slot_of = owner_of * CAP + before_me
    turned_books = codebooks.T
    unit, inverse = unit_rows(local_codes, codebooks)
    inverse_wide = jnp.broadcast_to(inverse, (inverse.shape[0], LANES))

    units, queries, stats, codes = call(
        stats_kernel,
        (
            sds((cols, feat), BF16),
            sds((all_rows, feat), BF16),
            sds((8, all_rows), F32),
            sds((BOOKS, cols), F32),
        ),
        [pltpu.VMEM((owners * BOOKS, LANES), F32), pltpu.VMEM((cols, LANES), jnp.int32)],
        2,
        7,
        2 * cols * feat * (BOOKS * CODES + all_rows),
    )(wanted, place, arrived.reshape(owners * BOOKS, LANES), *query_parts, tkey, turned_books)

    near = [(i, i ^ 1) for i in range(reps)]
    cross = [(i, reps - 1 - i) for i in range(reps)]
    peak, total, hit = merged(stats, lax.ppermute(stats, "rep", near))
    stats_two = jnp.concatenate(
        [peak, total, hit, jnp.zeros((5, all_rows), F32)], axis=0
    )
    stats_far = lax.ppermute(stats_two, "rep", cross)

    outbound, grad_cols, loss, own_t, far1, far2, far3 = call(
        grads_kernel,
        (
            sds((owners * CAP, PR, feat), BF16),
            sds((cols, feat), F32),
            sds((1, row_count), F32),
            sds((feat, row_count), F32),
            *[sds((feat, row_count), BF16)] * 3,
        ),
        [
            pltpu.VMEM((cols, LANES), jnp.int32),
            pltpu.VMEM((8, all_rows), F32),
            pltpu.VMEM((feat, all_rows), F32),
        ],
        3,
        5,
        6 * cols * feat * all_rows,
    )(wanted, slot_of, place, stats_two, stats_far, tkey, units, queries)

    outbound = outbound.reshape(owners, CAP * PR, feat)
    returned = lax.all_to_all(outbound, BLK, 0, 0, tiled=True)
    returned = returned.reshape(owners * CAP, PR, feat)

    query_grad_t = own_t
    for k, part in enumerate((far1, far2, far3)):
        query_grad_t = query_grad_t + shifted(part, k + 1).astype(F32)

    chunk_rows = codebooks.shape[0] // (x_count * z_count)
    keep, send = call(
        books_kernel,
        (
            sds((x_count * z_count, chunk_rows // 2, feat), F32),
            sds((x_count * z_count, chunk_rows // 2, feat), BF16),
        ),
        [pltpu.VMEM((BOOKS, CODES, cols), BF16), pltpu.VMEM((BOOKS * CODES, feat), F32)],
        1,
        3,
        4 * cols * feat * BOOKS * CODES,
    )(place, codes, turned_books, grad_cols)
    other = lax.ppermute(send, "c", [(0, 1), (1, 0)])
    share_rows = chunk_rows // 2 // reps
    share = (x_count * z_count, share_rows, feat)
    mine, *parts = call(
        deal_kernel,
        (sds(share, F32), *[sds(share, BF16)] * 3),
        [pltpu.VMEM((x_count * z_count, chunk_rows // 2, feat), F32)],
        1,
        2,
        cols * feat,
    )(place, keep, other)
    for k, part in enumerate(parts):
        mine = mine + shifted(part, k + 1).astype(F32)
    mine = halved(mine, "x", lambda i: i ^ 1)
    mine = halved(mine, "x", lambda i: x_count - 1 - i)
    bit = z_count // 2
    while bit:
        mine = halved(mine, "z", lambda i, bit=bit: i ^ bit)
        bit //= 2
    codebook_grad = mine.reshape(share_rows, feat)

    directory = arrived[:, 0, held : held + pair_count].astype(jnp.int32)
    local_iota = jnp.arange(PBLK_DEV, dtype=jnp.int32)
    named = jnp.any(
        directory[:, :, None] == here_blk * PBLK_DEV + local_iota[None, None, :], axis=1
    )
    slot_j = []
    for k in range(CAP):
        rank = jnp.zeros((owners,), jnp.int32)
        found = jnp.full((owners,), PBLK_DEV, jnp.int32)
        for j in range(PBLK_DEV):
            found = jnp.where(named[:, j] & (rank == k), j, found)
            rank = rank + named[:, j].astype(jnp.int32)
        slot_j.append(found)
    slot_j = jnp.stack(slot_j, axis=1).reshape(-1)
    passage_grad = call(
        return_kernel,
        sds((PBLK_DEV * PR, feat), F32),
        [pltpu.VMEM((PBLK_DEV + 1, PR, feat), F32) for _ in range(4)],
        1,
        3,
        owners * CAP * PR * feat,
    )(slot_j, returned, unit, inverse_wide)
    return (
        loss[None],
        query_grad_t.T[None, None],
        passage_grad[None, None],
        codebook_grad,
    )


def solution(mesh):
    reps = mesh.shape["rep"]
    torus = Mesh(mesh.devices.reshape(4, -1, 2, reps), AXES)
    in_specs = (
        P(BLK, "rep", None, None),
        P(BLK, None, None),
        P(BLK, None),
        P(BLK, "rep", None, None),
        P(),
    )
    out_specs = (
        P(BLK, "rep", None),
        P(BLK, "rep", None, None),
        P(BLK, "rep", None, None),
        P(AXES, None),
    )
    return jax.shard_map(
        shards, mesh=torus, in_specs=in_specs, out_specs=out_specs, check_vma=False
    )
```

```python
import functools

import jax
import jax.numpy as jnp
from jax import lax
from jax.experimental import pallas as pl
from jax.experimental.pallas import tpu as pltpu
from jax.sharding import Mesh
from jax.sharding import PartitionSpec as P


CODES = 256
BOOKS = 8
PR = 16
PBLK_DEV = 4
CAP = 2
LANES = 128
AXES = ("x", "z", "c", "rep")
BLK = ("x", "z", "c")
EPS = 1e-06
INTERPRET = False
VMEM_LIMIT = 24 << 20

F32 = jnp.float32
BF16 = jnp.bfloat16
VMEM = pl.BlockSpec(memory_space=pltpu.VMEM)
SMEM = pl.BlockSpec(memory_space=pltpu.SMEM)
CONTRACT_LAST = (((1,), (1,)), ((), ()))
CONTRACT_FIRST = (((0,), (0,)), ((), ()))


def call(kernel, out_shape, scratch, smem_count, vmem_count, flops):
    out_bytes = sum(s.size * s.dtype.itemsize for s in jax.tree.leaves(out_shape))
    return pl.pallas_call(
        kernel,
        out_shape=out_shape,
        in_specs=[SMEM] * smem_count + [VMEM] * vmem_count,
        out_specs=jax.tree.map(lambda _: VMEM, out_shape),
        scratch_shapes=scratch,
        interpret=INTERPRET,
        compiler_params=pltpu.CompilerParams(vmem_limit_bytes=VMEM_LIMIT),
        cost_estimate=pl.CostEstimate(
            flops=flops, bytes_accessed=2 * out_bytes, transcendentals=0
        ),
    )


def sds(shape, dtype):
    return jax.ShapeDtypeStruct(shape, dtype)


def one_hot_of(codes_ref, book, rows):
    cols = codes_ref.shape[1]
    row = codes_ref[book : book + 1, :]
    iota = lax.broadcasted_iota(jnp.int32, (rows, cols), 0).astype(F32)
    return jnp.where(row == iota, 1.0, 0.0).astype(BF16)


def fill_keys(pair_s, key_ref, pair_count):
    sub = lax.broadcasted_iota(jnp.int32, (PR, LANES), 0)
    for slot in range(pair_count):
        key_ref[slot * PR : (slot + 1) * PR, :] = sub + pair_s[slot] * PR


def hits(key_ref, start, count, tkey_ref):
    keys = key_ref[start : start + count, :]
    width = tkey_ref.shape[1]
    wide = jnp.concatenate([keys] * (width // LANES), axis=1)
    return wide == tkey_ref[...]


def stats_kernel(
    pair_s, place_s, recv_ref, q0, q1, q2, q3, tkey_ref, cbt_ref,
    u_ref, q_ref, st_ref, codes_ref, unit_ref, inv_ref, rows_ref, key_ref,
):
    cols = u_ref.shape[0]
    pair_count = cols // PR
    rep = place_s[3]
    rows = q0.shape[0]
    parts = (q0, q1, q2, q3)
    for k in range(len(parts)):
        owner = lax.rem(rep + len(parts) - k, len(parts))
        q_ref[pl.ds(pl.multiple_of(owner * rows, rows), rows), :] = parts[k][...]
    rows_ref[...] = recv_ref[...].astype(F32)
    lane_group = lax.broadcasted_iota(jnp.int32, (BOOKS, LANES), 1) // PR
    per_tile = LANES // PR
    for tile in range(cols // LANES):
        held = jnp.zeros((BOOKS, LANES), F32)
        for place in range(per_tile):
            block = pair_s[tile * per_tile + place]
            owner = block >> 2
            within = block & 3
            codes = rows_ref[pl.ds(pl.multiple_of(owner * BOOKS, BOOKS), BOOKS), :]
            turned = pltpu.roll(codes, lax.rem(LANES + (place - within) * PR, LANES), axis=1)
            held = jnp.where(lane_group == place, turned, held)
        codes_ref[:, tile * LANES : (tile + 1) * LANES] = held
    fill_keys(pair_s, key_ref, pair_count)
    quant = jnp.zeros((cbt_ref.shape[0], cols), F32)
    for book in range(BOOKS):
        quant = quant + jnp.dot(
            cbt_ref[:, book * CODES : (book + 1) * CODES],
            one_hot_of(codes_ref, book, CODES),
            preferred_element_type=F32,
        )
    inverse = lax.rsqrt(jnp.sum(quant * quant, axis=0, keepdims=True) + EPS)
    unit = quant * inverse
    unit_ref[...] = unit
    inv_ref[...] = inverse
    u_ref[...] = unit.T.astype(BF16)
    total_rows = q_ref.shape[0]
    peak = jnp.full((1, total_rows), -1e30, F32)
    total = jnp.zeros((1, total_rows), F32)
    hit = jnp.zeros((1, total_rows), F32)
    step = min(256, cols)
    for start in range(0, cols, step):
        scores = lax.dot_general(
            u_ref[start : start + step, :], q_ref[...], CONTRACT_LAST, preferred_element_type=F32
        )
        fresh = jnp.maximum(peak, jnp.max(scores, axis=0, keepdims=True))
        total = total * jnp.exp(peak - fresh) + jnp.sum(
            jnp.exp(scores - fresh), axis=0, keepdims=True
        )
        peak = fresh
        hit = hit + jnp.sum(
            jnp.where(hits(key_ref, start, step, tkey_ref), scores, 0.0), axis=0, keepdims=True
        )
    st_ref[0:1, :] = peak
    st_ref[1:2, :] = total
    st_ref[2:3, :] = hit


def hot_kernel(codes_ref, hot_ref):
    for book in range(BOOKS):
        hot_ref[book] = one_hot_of(codes_ref, book, CODES)


def pack_kernel(codes_ref, pairs_ref, out_ref):
    codes = codes_ref[...]
    spare = LANES - codes.shape[1] - pairs_ref.shape[1]
    pieces = [codes, jnp.broadcast_to(pairs_ref[...], (BOOKS, pairs_ref.shape[1]))]
    if spare:
        pieces.append(jnp.zeros((BOOKS, spare), jnp.int32))
    message = jnp.concatenate(pieces, axis=1).astype(F32).astype(BF16)
    for peer in range(out_ref.shape[0]):
        out_ref[peer] = message


def merged(first, second):
    peak = jnp.maximum(first[0:1], second[0:1])
    total = first[1:2] * jnp.exp(first[0:1] - peak) + second[1:2] * jnp.exp(second[0:1] - peak)
    return peak, total, first[2:3] + second[2:3]


def grads_kernel(
    pair_s, slot_s, place_s, sta_ref, stb_ref, tkey_ref, u_ref, q_ref, unit_ref, inv_ref, hot_ref,
    send_ref, loss_ref, own_ref, far1, far2, far3, keep_ref, give_ref,
    key_ref, lse_ref, qgt_ref, pg_ref, sum_ref,
):
    cols = u_ref.shape[0]
    pair_count = cols // PR
    core, rep = place_s[2], place_s[3]
    rows = own_ref.shape[1]
    peak, total, hit = merged(sta_ref[...], stb_ref[...])
    lse = peak + jnp.log(total)
    lse_ref[0:1, :] = lse - hit
    loss_ref[...] = lse_ref[0:1, pl.ds(pl.multiple_of(rep * rows, rows), rows)]
    fill_keys(pair_s, key_ref, pair_count)
    send_ref[...] = jnp.zeros(send_ref.shape, BF16)
    step = min(256, cols)
    grown = None
    for start in range(0, cols, step):
        span = slice(start, start + step)
        u_part = u_ref[span, :]
        scores = lax.dot_general(u_part, q_ref[...], CONTRACT_LAST, preferred_element_type=F32)
        hit_mask = hits(key_ref, start, step, tkey_ref)
        weight = (jnp.exp(scores - lse) - jnp.where(hit_mask, 1.0, 0.0)).astype(BF16)
        grad = jnp.dot(weight, q_ref[...], preferred_element_type=F32)
        narrow = grad.astype(BF16)
        for place in range(step // PR):
            send_ref[slot_s[start // PR + place]] = narrow[place * PR : (place + 1) * PR, :]
        turned = grad.T
        unit = unit_ref[:, span]
        along = jnp.sum(unit * turned, axis=0, keepdims=True)
        pg_ref[:, span] = (inv_ref[0:1, span] * (turned - unit * along)).astype(BF16)
        term = lax.dot_general(u_part, weight, CONTRACT_FIRST, preferred_element_type=F32)
        grown = term if grown is None else grown + term
    qgt_ref[...] = grown
    count = q_ref.shape[0] // rows
    for k, out in enumerate((own_ref, far1, far2, far3)):
        owner = lax.rem(rep + k, count)
        part = qgt_ref[:, pl.ds(pl.multiple_of(owner * rows, rows), rows)]
        out[...] = part.astype(out.dtype)
    for book in range(BOOKS):
        sum_ref[book * CODES : (book + 1) * CODES, :] = lax.dot_general(
            hot_ref[book], pg_ref[...], CONTRACT_LAST, preferred_element_type=F32
        )
    half = keep_ref.shape[1]
    for chunk in range(keep_ref.shape[0]):
        base = chunk * 2 * half
        keep_ref[chunk] = sum_ref[pl.ds(pl.multiple_of(base + core * half, half), half), :]
        give_ref[chunk] = sum_ref[
            pl.ds(pl.multiple_of(base + (1 - core) * half, half), half), :
        ].astype(BF16)


def x_partners(count):
    if count == 4:
        return [lambda i: i ^ 1, lambda i: 3 - i]
    return [lambda i: i ^ 1][: count - 1]


def z_partners(count):
    if count == 8:
        return [
            lambda i: (i + 3 - 6 * (i & 1)) & 7,
            lambda i: (i - 1 + 2 * (i & 1)) & 7,
            lambda i: i ^ 1,
        ]
    return [lambda i: i ^ 1][: count - 1]


def halving_order(here, partners):
    order = [here]
    for partner in reversed(partners):
        order = order + halving_tail(partner(here), partners, len(order))
    return order


def halving_tail(there, partners, length):
    order = [there]
    for partner in reversed(partners):
        if len(order) == length:
            break
        order = order + halving_tail(partner(there), partners, len(order))
    return order


def deal_kernel(place_s, keep_ref, recv_ref, qg1, qg2, qg3, own_ref, far1, far2, far3, sum_ref, *, sizes):
    x_here, z_here, rep = place_s[0], place_s[1], place_s[3]
    x_count, z_count, reps = sizes
    share = keep_ref.shape[1] // reps
    sum_ref[...] = keep_ref[...] + recv_ref[...].astype(F32)
    order = [
        px * z_count + pz
        for px in halving_order(x_here, x_partners(x_count))
        for pz in halving_order(z_here, z_partners(z_count))
    ]
    for k, out in enumerate((own_ref, far1, far2, far3)):
        owner = lax.rem(rep + k, reps)
        at = pl.ds(pl.multiple_of(owner * share, share), share)
        for pair in range(len(order) // 2):
            rows = jnp.concatenate(
                [sum_ref[order[2 * pair], at, :], sum_ref[order[2 * pair + 1], at, :]], axis=0
            )
            out[2 * pair * share : (2 * pair + 2) * share, :] = rows.astype(out.dtype)
    dealt = len(order) * share
    for out, part in zip((far1, far2, far3), (qg1, qg2, qg3)):
        out[dealt : dealt + part.shape[0], :] = part[...]


def return_kernel(slot_j, ret_ref, unit_ref, inv_ref, book_ref, more_ref, out_ref, total_ref, *sums):
    total_ref[...] = book_ref[...] + more_ref[...].astype(F32)
    for part in sums:
        part[...] = jnp.zeros(part.shape, F32)
    for slot in range(ret_ref.shape[0]):
        part = sums[slot % len(sums)]
        j = slot_j[slot]
        part[j] = part[j] + ret_ref[slot].astype(F32)
    for j in range(PBLK_DEV):
        grad = sums[0][j]
        for part in sums[1:]:
            grad = grad + part[j]
        unit = unit_ref[j * PR : (j + 1) * PR, :]
        inverse = inv_ref[j * PR : (j + 1) * PR, 0:1]
        out_ref[j * PR : (j + 1) * PR, :] = inverse * (
            grad - unit * jnp.sum(unit * grad, axis=1, keepdims=True)
        )


def unit_rows(local_codes, codebooks):
    iota = jnp.arange(CODES, dtype=jnp.int32)
    pieces = [
        (local_codes[book][:, None] == iota[None, :]).astype(BF16)
        for book in range(local_codes.shape[0])
    ]
    quant = jnp.dot(jnp.concatenate(pieces, axis=1), codebooks, preferred_element_type=F32)
    inverse = lax.rsqrt(jnp.sum(quant * quant, axis=1, keepdims=True) + EPS)
    return (quant * inverse, inverse)


def shifted(x, k):
    count = lax.axis_size("rep")
    return lax.ppermute(x, "rep", [(i, (i + k) % count) for i in range(count)])


def halved(own, axis, partner):
    half = own.shape[0] // 2
    pairs = [(i, partner(i)) for i in range(lax.axis_size(axis))]
    return own[:half], lax.ppermute(own[half:].astype(BF16), axis, pairs)


def shards(query_embed, positive_ids, pair_blocks, code_ids, codebooks):
    reps = lax.axis_size("rep")
    x_count, z_count, cores = (lax.axis_size(a) for a in BLK)
    owners = x_count * z_count * cores
    here_blk = lax.axis_index(BLK)
    here_rep = lax.axis_index("rep")
    rows_mine = query_embed[0, 0]
    row_count, feat = rows_mine.shape
    all_rows = reps * row_count
    wanted = pair_blocks[0]
    pair_count = wanted.shape[0]
    cols = pair_count * PR
    local_codes = code_ids[0, 0]
    place = jnp.stack([lax.axis_index(a) for a in AXES]).astype(jnp.int32)

    held = local_codes.shape[1]
    message = call(
        pack_kernel, sds((owners, BOOKS, LANES), BF16), [], 0, 2, owners * BOOKS * LANES
    )(local_codes, wanted[None, :])
    arrived = lax.all_to_all(message, BLK, 0, 0, tiled=True)
    query_parts = [rows_mine] + [shifted(rows_mine, k) for k in range(1, reps)]

    targets = positive_ids[0].reshape(1, all_rows)
    row_in = targets % (PR * reps)
    tkey = jnp.where(
        row_in // PR == here_rep, (targets // (PR * reps)) * PR + row_in % PR, -1
    ).astype(jnp.int32)
    owner_of = wanted // PBLK_DEV
    before_me = jnp.sum(
        ((owner_of[None, :] == owner_of[:, None]) & (wanted[None, :] < wanted[:, None])).astype(
            jnp.int32
        ),
        axis=1,
    )
    slot_of = owner_of * CAP + before_me
    turned_books = codebooks.T
    unit, inverse = unit_rows(local_codes, codebooks)
    inverse_wide = jnp.broadcast_to(inverse, (inverse.shape[0], LANES))

    units, queries, stats, codes, unit_t, inv_t = call(
        stats_kernel,
        (
            sds((cols, feat), BF16),
            sds((all_rows, feat), BF16),
            sds((3, all_rows), F32),
            sds((BOOKS, cols), F32),
            sds((feat, cols), F32),
            sds((1, cols), F32),
        ),
        [pltpu.VMEM((owners * BOOKS, LANES), F32), pltpu.VMEM((cols, LANES), jnp.int32)],
        2,
        7,
        2 * cols * feat * (BOOKS * CODES + all_rows),
    )(wanted, place, arrived.reshape(owners * BOOKS, LANES), *query_parts, tkey, turned_books)

    near = [(i, i ^ 1) for i in range(reps)]
    cross = [(i, reps - 1 - i) for i in range(reps)]
    stats_near = lax.ppermute(stats, "rep", near)
    hot = call(hot_kernel, sds((BOOKS, CODES, cols), BF16), [], 0, 1, BOOKS * CODES * cols)(codes)
    stats_two = jnp.concatenate(merged(stats, stats_near), axis=0)
    stats_far = lax.ppermute(stats_two, "rep", cross)

    chunks = x_count * z_count
    chunk_rows = codebooks.shape[0] // chunks
    half_rows = chunk_rows // cores
    outbound, loss, own_t, far1, far2, far3, keep, give = call(
        grads_kernel,
        (
            sds((owners * CAP, PR, feat), BF16),
            sds((1, row_count), F32),
            sds((feat, row_count), F32),
            *[sds((feat, row_count), BF16)] * 3,
            sds((chunks, half_rows, feat), F32),
            sds((chunks, half_rows, feat), BF16),
        ),
        [
            pltpu.VMEM((cols, LANES), jnp.int32),
            pltpu.VMEM((8, all_rows), F32),
            pltpu.VMEM((feat, all_rows), F32),
            pltpu.VMEM((feat, cols), BF16),
            pltpu.VMEM((BOOKS * CODES, feat), F32),
        ],
        3,
        8,
        cols * feat * (6 * all_rows + 2 * BOOKS * CODES),
    )(wanted, slot_of, place, stats_two, stats_far, tkey, units, queries, unit_t, inv_t, hot)

    outbound = outbound.reshape(owners, CAP * PR, feat)
    returned = lax.all_to_all(outbound, BLK, 0, 0, tiled=True)
    returned = returned.reshape(owners * CAP, PR, feat)

    other = lax.ppermute(give, "c", [(0, 1), (1, 0)])
    share_rows = half_rows // reps
    dealt = chunks * share_rows
    mine, *parts = call(
        functools.partial(deal_kernel, sizes=(x_count, z_count, reps)),
        (sds((dealt, feat), F32), *[sds((dealt + feat, row_count), BF16)] * 3),
        [pltpu.VMEM((chunks, half_rows, feat), F32)],
        1,
        5,
        cols * feat,
    )(place, keep, other, far1, far2, far3)
    parts = [shifted(part, k + 1) for k, part in enumerate(parts)]
    query_grad_t = own_t
    for part in parts:
        mine = mine + part[:dealt].astype(F32)
        query_grad_t = query_grad_t + part[dealt:].astype(F32)
    steps = [("x", partner) for partner in x_partners(x_count)]
    steps += [("z", partner) for partner in z_partners(z_count)]
    for axis, partner in steps[:-1]:
        kept, more = halved(mine, axis, partner)
        mine = kept + more.astype(F32)
    book_kept, book_more = halved(mine, *steps[-1])

    directory = arrived[:, 0, held : held + pair_count].astype(jnp.int32)
    local_iota = jnp.arange(PBLK_DEV, dtype=jnp.int32)
    named = jnp.any(
        directory[:, :, None] == here_blk * PBLK_DEV + local_iota[None, None, :], axis=1
    )
    slot_j = []
    for k in range(CAP):
        rank = jnp.zeros((owners,), jnp.int32)
        found = jnp.full((owners,), PBLK_DEV, jnp.int32)
        for j in range(PBLK_DEV):
            found = jnp.where(named[:, j] & (rank == k), j, found)
            rank = rank + named[:, j].astype(jnp.int32)
        slot_j.append(found)
    slot_j = jnp.stack(slot_j, axis=1).reshape(-1)
    passage_grad, codebook_grad = call(
        return_kernel,
        (sds((PBLK_DEV * PR, feat), F32), sds((share_rows, feat), F32)),
        [pltpu.VMEM((PBLK_DEV + 1, PR, feat), F32) for _ in range(4)],
        1,
        5,
        owners * CAP * PR * feat,
    )(slot_j, returned, unit, inverse_wide, book_kept, book_more)
    return (
        loss[None],
        query_grad_t.T[None, None],
        passage_grad[None, None],
        codebook_grad,
    )


def solution(mesh):
    reps = mesh.shape["rep"]
    torus = Mesh(mesh.devices.reshape(4, -1, 2, reps), AXES)
    in_specs = (
        P(BLK, "rep", None, None),
        P(BLK, None, None),
        P(BLK, None),
        P(BLK, "rep", None, None),
        P(),
    )
    out_specs = (
        P(BLK, "rep", None),
        P(BLK, "rep", None, None),
        P(BLK, "rep", None, None),
        P(AXES, None),
    )
    return jax.shard_map(
        shards, mesh=torus, in_specs=in_specs, out_specs=out_specs, check_vma=False
    )
```

```python
import functools

import jax
import jax.numpy as jnp
from jax import lax
from jax.experimental import pallas as pl
from jax.experimental.pallas import tpu as pltpu
from jax.sharding import Mesh
from jax.sharding import PartitionSpec as P


CODES = 256
BOOKS = 8
PR = 16
PBLK_DEV = 4
CAP = 2
LANES = 128
AXES = ("x", "z", "c", "rep")
BLK = ("x", "z", "c")
EPS = 1e-06
INTERPRET = False
VMEM_LIMIT = 24 << 20
WHOLE_VMEM = 63_000_000

F32 = jnp.float32
BF16 = jnp.bfloat16
VMEM = pl.BlockSpec(memory_space=pltpu.VMEM)
SMEM = pl.BlockSpec(memory_space=pltpu.SMEM)
HBM = pl.BlockSpec(memory_space=pltpu.HBM)
CONTRACT_LAST = (((1,), (1,)), ((), ()))
CONTRACT_FIRST = (((0,), (0,)), ((), ()))


def call(kernel, out_shape, scratch, smem_count, vmem_count, flops, hbm_count=0,
         limit=VMEM_LIMIT):
    out_bytes = sum(s.size * s.dtype.itemsize for s in jax.tree.leaves(out_shape))
    return pl.pallas_call(
        kernel,
        out_shape=out_shape,
        in_specs=[SMEM] * smem_count + [HBM] * hbm_count + [VMEM] * vmem_count,
        out_specs=jax.tree.map(lambda _: VMEM, out_shape),
        scratch_shapes=scratch,
        interpret=INTERPRET,
        compiler_params=pltpu.CompilerParams(vmem_limit_bytes=limit),
        cost_estimate=pl.CostEstimate(
            flops=flops, bytes_accessed=2 * out_bytes, transcendentals=0
        ),
    )


def sds(shape, dtype):
    return jax.ShapeDtypeStruct(shape, dtype)


def one_hot_of(codes_ref, book, rows):
    cols = codes_ref.shape[1]
    row = codes_ref[book : book + 1, :]
    iota = lax.broadcasted_iota(jnp.int32, (rows, cols), 0).astype(F32)
    return jnp.where(row == iota, 1.0, 0.0).astype(BF16)


def fill_keys(pair_s, key_ref, pair_count):
    sub = lax.broadcasted_iota(jnp.int32, (PR, LANES), 0)
    for slot in range(pair_count):
        key_ref[slot * PR : (slot + 1) * PR, :] = sub + pair_s[0, slot] * PR


def hits(key_ref, start, count, tkey_ref):
    keys = key_ref[start : start + count, :]
    width = tkey_ref.shape[1]
    wide = jnp.concatenate([keys] * (width // LANES), axis=1)
    return wide == tkey_ref[...]


def stats_kernel(
    pair_s, place_s, recv_ref, near_ref, far_ref, tkey_ref, cbt_ref,
    u_ref, q_ref, st_ref, codes_ref, unit_ref, inv_ref, rows_ref, key_ref,
):
    cols = u_ref.shape[0]
    pair_count = cols // PR
    rep = place_s[3]
    rows = near_ref.shape[0] // 2
    across = q_ref.shape[0] // rows - 1 - rep
    for owner, part in (
        (rep, near_ref[0:rows, :]),
        (rep ^ 1, near_ref[rows : 2 * rows, :]),
        (across, far_ref[0:rows, :]),
        (across ^ 1, far_ref[rows : 2 * rows, :]),
    ):
        q_ref[pl.ds(pl.multiple_of(owner * rows, rows), rows), :] = part
    rows_ref[...] = recv_ref[...].astype(F32)
    lane_group = lax.broadcasted_iota(jnp.int32, (BOOKS, LANES), 1) // PR
    per_tile = LANES // PR
    for tile in range(cols // LANES):
        held = jnp.zeros((BOOKS, LANES), F32)
        for place in range(per_tile):
            block = pair_s[0, tile * per_tile + place]
            owner = block >> 2
            within = block & 3
            codes = rows_ref[pl.ds(pl.multiple_of(owner * BOOKS, BOOKS), BOOKS), :]
            turned = pltpu.roll(codes, lax.rem(LANES + (place - within) * PR, LANES), axis=1)
            held = jnp.where(lane_group == place, turned, held)
        codes_ref[:, tile * LANES : (tile + 1) * LANES] = held
    fill_keys(pair_s, key_ref, pair_count)
    quant = jnp.zeros((cbt_ref.shape[0], cols), F32)
    for book in range(BOOKS):
        quant = quant + jnp.dot(
            cbt_ref[:, book * CODES : (book + 1) * CODES],
            one_hot_of(codes_ref, book, CODES),
            preferred_element_type=F32,
        )
    inverse = lax.rsqrt(jnp.sum(quant * quant, axis=0, keepdims=True) + EPS)
    unit = quant * inverse
    unit_ref[...] = unit
    inv_ref[...] = inverse
    u_ref[...] = unit.T.astype(BF16)
    total_rows = q_ref.shape[0]
    peak = jnp.full((1, total_rows), -1e30, F32)
    total = jnp.zeros((1, total_rows), F32)
    hit = jnp.zeros((1, total_rows), F32)
    step = min(256, cols)
    for start in range(0, cols, step):
        scores = lax.dot_general(
            u_ref[start : start + step, :], q_ref[...], CONTRACT_LAST, preferred_element_type=F32
        )
        fresh = jnp.maximum(peak, jnp.max(scores, axis=0, keepdims=True))
        total = total * jnp.exp(peak - fresh) + jnp.sum(
            jnp.exp(scores - fresh), axis=0, keepdims=True
        )
        peak = fresh
        hit = hit + jnp.sum(
            jnp.where(hits(key_ref, start, step, tkey_ref), scores, 0.0), axis=0, keepdims=True
        )
    st_ref[0:1, :] = peak
    st_ref[1:2, :] = total
    st_ref[2:3, :] = hit


def hot_kernel(codes_ref, hot_ref):
    for book in range(BOOKS):
        hot_ref[book] = one_hot_of(codes_ref, book, CODES)


def pack_kernel(codes_hbm, pairs_hbm, out_ref, codes_ref, pairs_ref, sems):
    copies = [
        pltpu.make_async_copy(codes_hbm, codes_ref, sems.at[0]),
        pltpu.make_async_copy(pairs_hbm, pairs_ref, sems.at[1]),
    ]
    for copy in copies:
        copy.start()
    for copy in copies:
        copy.wait()
    codes = codes_ref[...]
    spare = LANES - codes.shape[1] - pairs_ref.shape[1]
    pieces = [codes, jnp.broadcast_to(pairs_ref[...], (BOOKS, pairs_ref.shape[1]))]
    if spare:
        pieces.append(jnp.zeros((BOOKS, spare), jnp.int32))
    message = jnp.concatenate(pieces, axis=1).astype(F32).astype(BF16)
    for peer in range(out_ref.shape[0]):
        out_ref[peer] = message


def side_kernel(
    place_s, codes_hbm, pairs_hbm, targets_hbm, books_hbm,
    pairs_ref, slot_ref, tkey_ref, cbt_ref, unit_ref, inv_ref,
    codes_ref, near_ref, targets_ref, books_ref, float_ref, sems,
):
    moves = (
        (codes_hbm, codes_ref),
        (pairs_hbm, near_ref),
        (targets_hbm, targets_ref),
        (books_hbm, books_ref),
    )
    copies = [pltpu.make_async_copy(a, b, sems.at[k]) for k, (a, b) in enumerate(moves)]
    for copy in copies:
        copy.start()
    for copy in copies:
        copy.wait()
    rep = place_s[3]
    pairs_ref[...] = near_ref[...]
    count = near_ref.shape[1]
    wide = jnp.broadcast_to(near_ref[...], (count, count))
    tall = wide.astype(F32).T.astype(jnp.int32)
    before = ((tall >> 2) == (wide >> 2)) & (tall < wide)
    slot_ref[...] = (near_ref[...] >> 2) * CAP + jnp.sum(
        jnp.where(before, 1, 0), axis=0, keepdims=True
    )
    reps, rows = targets_ref.shape
    for k in range(reps):
        target = targets_ref[k : k + 1, :]
        block = target // (PR * reps)
        within = target - block * (PR * reps)
        mine = within // PR == rep
        tkey_ref[:, k * rows : (k + 1) * rows] = jnp.where(
            mine, block * PR + within - rep * PR, -1
        )
    float_ref[...] = codes_ref[...].astype(F32)
    quant = jnp.zeros(unit_ref.shape, F32)
    for book in range(BOOKS):
        span = slice(book * CODES, (book + 1) * CODES)
        words = books_ref[span, :]
        cbt_ref[:, span] = words.T
        quant = quant + lax.dot_general(
            one_hot_of(float_ref, book, CODES), words, CONTRACT_FIRST, preferred_element_type=F32
        )
    inverse = lax.rsqrt(jnp.sum(quant * quant, axis=1, keepdims=True) + EPS)
    unit_ref[...] = quant * inverse
    inv_ref[...] = jnp.broadcast_to(inverse, inv_ref.shape)


def merged(first, second):
    peak = jnp.maximum(first[0:1], second[0:1])
    total = first[1:2] * jnp.exp(first[0:1] - peak) + second[1:2] * jnp.exp(second[0:1] - peak)
    return peak, total, first[2:3] + second[2:3]


def grads_kernel(
    pair_s, slot_s, place_s, sta_ref, stb_ref, tkey_ref, u_ref, q_ref, unit_ref, inv_ref, hot_ref,
    send_ref, loss_ref, own_ref, far1, far2, far3, keep_ref, give_ref,
    key_ref, lse_ref, qgt_ref, pg_ref, sum_ref,
):
    cols = u_ref.shape[0]
    pair_count = cols // PR
    core, rep = place_s[2], place_s[3]
    rows = own_ref.shape[1]
    peak, total, hit = merged(sta_ref[...], stb_ref[...])
    lse = peak + jnp.log(total)
    lse_ref[0:1, :] = lse - hit
    loss_ref[...] = lse_ref[0:1, pl.ds(pl.multiple_of(rep * rows, rows), rows)]
    fill_keys(pair_s, key_ref, pair_count)
    send_ref[...] = jnp.zeros(send_ref.shape, BF16)
    step = min(256, cols)
    grown = None
    for start in range(0, cols, step):
        span = slice(start, start + step)
        u_part = u_ref[span, :]
        scores = lax.dot_general(u_part, q_ref[...], CONTRACT_LAST, preferred_element_type=F32)
        hit_mask = hits(key_ref, start, step, tkey_ref)
        weight = (jnp.exp(scores - lse) - jnp.where(hit_mask, 1.0, 0.0)).astype(BF16)
        grad = jnp.dot(weight, q_ref[...], preferred_element_type=F32)
        narrow = grad.astype(BF16)
        for place in range(step // PR):
            send_ref[slot_s[0, start // PR + place]] = narrow[place * PR : (place + 1) * PR, :]
        turned = grad.T
        unit = unit_ref[:, span]
        along = jnp.sum(unit * turned, axis=0, keepdims=True)
        pg_ref[:, span] = (inv_ref[0:1, span] * (turned - unit * along)).astype(BF16)
        term = lax.dot_general(u_part, weight, CONTRACT_FIRST, preferred_element_type=F32)
        grown = term if grown is None else grown + term
    qgt_ref[...] = grown
    count = q_ref.shape[0] // rows
    for k, out in enumerate((own_ref, far1, far2, far3)):
        owner = lax.rem(rep + k, count)
        part = qgt_ref[:, pl.ds(pl.multiple_of(owner * rows, rows), rows)]
        out[...] = part.astype(out.dtype)
    for book in range(BOOKS):
        sum_ref[book * CODES : (book + 1) * CODES, :] = lax.dot_general(
            hot_ref[book], pg_ref[...], CONTRACT_LAST, preferred_element_type=F32
        )
    half = keep_ref.shape[1]
    for chunk in range(keep_ref.shape[0]):
        base = chunk * 2 * half
        keep_ref[chunk] = sum_ref[pl.ds(pl.multiple_of(base + core * half, half), half), :]
        give_ref[chunk] = sum_ref[
            pl.ds(pl.multiple_of(base + (1 - core) * half, half), half), :
        ].astype(BF16)


def x_partners(count):
    if count == 4:
        return [lambda i: i ^ 1, lambda i: 3 - i]
    return [lambda i: i ^ 1][: count - 1]


def z_partners(count):
    if count == 8:
        return [
            lambda i: i ^ 1,
            lambda i: (i - 1 + 2 * (i & 1)) & 7,
            lambda i: (i + 3 - 6 * (i & 1)) & 7,
        ]
    return [lambda i: i ^ 1][: count - 1]


def halving_order(here, partners):
    order = [here]
    for partner in reversed(partners):
        order = order + halving_tail(partner(here), partners, len(order))
    return order


def halving_tail(there, partners, length):
    order = [there]
    for partner in reversed(partners):
        if len(order) == length:
            break
        order = order + halving_tail(partner(there), partners, len(order))
    return order


def split_kernel(place_s, keep_ref, recv_ref, stay_ref, give_ref, sum_ref, *, sizes):
    x_here, z_here = place_s[0], place_s[1]
    x_count, z_count = sizes
    half = z_count // 2
    sum_ref[...] = keep_ref[...] + recv_ref[...].astype(F32)
    z_order = halving_order(z_here, z_partners(z_count))
    for at, px in enumerate(halving_order(x_here, x_partners(x_count))):
        for k in range(half):
            stay_ref[at * half + k] = sum_ref[px * z_count + z_order[k]]
            give_ref[at * half + k] = sum_ref[px * z_count + z_order[half + k]].astype(BF16)


def deal_kernel(place_s, stay_ref, recv_ref, qg1, qg2, qg3, own_ref, far1, far2, far3, sum_ref):
    rep = place_s[3]
    chunks = stay_ref.shape[0]
    share = own_ref.shape[0] // chunks
    reps = stay_ref.shape[1] // share
    sum_ref[...] = stay_ref[...] + recv_ref[...].astype(F32)
    for k, out in enumerate((own_ref, far1, far2, far3)):
        owner = lax.rem(rep + k, reps)
        at = pl.ds(pl.multiple_of(owner * share, share), share)
        for pair in range(chunks // 2):
            rows = jnp.concatenate(
                [sum_ref[2 * pair, at, :], sum_ref[2 * pair + 1, at, :]], axis=0
            )
            out[2 * pair * share : (2 * pair + 2) * share, :] = rows.astype(out.dtype)
    dealt = own_ref.shape[0]
    for out, part in zip((far1, far2, far3), (qg1, qg2, qg3)):
        out[dealt : dealt + part.shape[0], :] = part[...]


def return_kernel(slot_j, ret_ref, unit_ref, inv_ref, out_ref, *sums):
    for part in sums:
        part[...] = jnp.zeros(part.shape, F32)
    for slot in range(ret_ref.shape[0]):
        part = sums[slot % len(sums)]
        j = slot_j[slot]
        part[j] = part[j] + ret_ref[slot].astype(F32)
    for j in range(PBLK_DEV):
        grad = sums[0][j]
        for part in sums[1:]:
            grad = grad + part[j]
        unit = unit_ref[j * PR : (j + 1) * PR, :]
        inverse = inv_ref[j * PR : (j + 1) * PR, 0:1]
        out_ref[j * PR : (j + 1) * PR, :] = inverse * (
            grad - unit * jnp.sum(unit * grad, axis=1, keepdims=True)
        )


def shifted(x, k):
    count = lax.axis_size("rep")
    return lax.ppermute(x, "rep", [(i, (i + k) % count) for i in range(count)])


def stepped(x, axis, partner):
    return lax.ppermute(x, axis, [(i, partner(i)) for i in range(lax.axis_size(axis))])


def shards(query_embed, positive_ids, pair_blocks, code_ids, codebooks):
    reps = lax.axis_size("rep")
    x_count, z_count, cores = (lax.axis_size(a) for a in BLK)
    owners = x_count * z_count * cores
    here_blk = lax.axis_index(BLK)
    rows_mine = query_embed[0, 0]
    row_count, feat = rows_mine.shape
    all_rows = reps * row_count
    wanted = pair_blocks[0]
    pair_count = wanted.shape[0]
    cols = pair_count * PR
    local_codes = code_ids[0, 0]
    place = jnp.stack([lax.axis_index(a) for a in AXES]).astype(jnp.int32)
    near = [(i, i ^ 1) for i in range(reps)]
    cross = [(i, reps - 1 - i) for i in range(reps)]
    pairs_in = wanted[None, :]
    held = local_codes.shape[1]

    rows_near = lax.ppermute(rows_mine, "rep", near)
    message = call(
        pack_kernel,
        sds((owners, BOOKS, LANES), BF16),
        [
            pltpu.VMEM((BOOKS, held), jnp.int32),
            pltpu.VMEM((1, pair_count), jnp.int32),
            pltpu.SemaphoreType.DMA((2,)),
        ],
        0,
        0,
        owners * BOOKS * LANES,
        2,
        WHOLE_VMEM,
    )(local_codes, pairs_in)
    arrived = lax.all_to_all(message, BLK, 0, 0, tiled=True)
    rows_pair = jnp.concatenate([rows_mine, rows_near], axis=0)
    rows_far = lax.ppermute(rows_pair, "rep", cross)
    pairs, slot_of, tkey, turned_books, unit, inverse_wide = call(
        side_kernel,
        (
            sds((1, pair_count), jnp.int32),
            sds((1, pair_count), jnp.int32),
            sds((1, all_rows), jnp.int32),
            sds((feat, BOOKS * CODES), BF16),
            sds((held, feat), F32),
            sds((held, LANES), F32),
        ),
        [
            pltpu.VMEM((BOOKS, held), jnp.int32),
            pltpu.VMEM((1, pair_count), jnp.int32),
            pltpu.VMEM((reps, row_count), jnp.int32),
            pltpu.VMEM((BOOKS * CODES, feat), BF16),
            pltpu.VMEM((BOOKS, held), F32),
            pltpu.SemaphoreType.DMA((4,)),
        ],
        1,
        0,
        2 * BOOKS * CODES * feat * held,
        4,
    )(place, local_codes, pairs_in, positive_ids[0], codebooks)

    units, queries, stats, codes, unit_t, inv_t = call(
        stats_kernel,
        (
            sds((cols, feat), BF16),
            sds((all_rows, feat), BF16),
            sds((3, all_rows), F32),
            sds((BOOKS, cols), F32),
            sds((feat, cols), F32),
            sds((1, cols), F32),
        ),
        [pltpu.VMEM((owners * BOOKS, LANES), F32), pltpu.VMEM((cols, LANES), jnp.int32)],
        2,
        5,
        2 * cols * feat * (BOOKS * CODES + all_rows),
    )(
        pairs, place, arrived.reshape(owners * BOOKS, LANES),
        rows_pair, rows_far, tkey, turned_books,
    )

    stats_near = lax.ppermute(stats, "rep", near)
    hot = call(hot_kernel, sds((BOOKS, CODES, cols), BF16), [], 0, 1, BOOKS * CODES * cols)(codes)
    stats_two = jnp.concatenate(merged(stats, stats_near), axis=0)
    stats_far = lax.ppermute(stats_two, "rep", cross)

    chunks = x_count * z_count
    chunk_rows = codebooks.shape[0] // chunks
    half_rows = chunk_rows // cores
    outbound, loss, own_t, far1, far2, far3, keep, give = call(
        grads_kernel,
        (
            sds((owners * CAP, PR, feat), BF16),
            sds((1, row_count), F32),
            sds((feat, row_count), F32),
            *[sds((feat, row_count), BF16)] * 3,
            sds((chunks, half_rows, feat), F32),
            sds((chunks, half_rows, feat), BF16),
        ),
        [
            pltpu.VMEM((cols, LANES), jnp.int32),
            pltpu.VMEM((8, all_rows), F32),
            pltpu.VMEM((feat, all_rows), F32),
            pltpu.VMEM((feat, cols), BF16),
            pltpu.VMEM((BOOKS * CODES, feat), F32),
        ],
        3,
        8,
        cols * feat * (6 * all_rows + 2 * BOOKS * CODES),
    )(pairs, slot_of, place, stats_two, stats_far, tkey, units, queries, unit_t, inv_t, hot)

    outbound = outbound.reshape(owners, CAP * PR, feat)
    returned = lax.all_to_all(outbound, BLK, 0, 0, tiled=True)
    returned = returned.reshape(owners * CAP, PR, feat)

    other = lax.ppermute(give, "c", [(0, 1), (1, 0)])
    steps = [("z", partner) for partner in z_partners(z_count)]
    steps = steps[:1] + [("x", partner) for partner in x_partners(x_count)] + steps[1:]
    held_chunks = chunks // 2
    stay, pass_on = call(
        functools.partial(split_kernel, sizes=(x_count, z_count)),
        (
            sds((held_chunks, half_rows, feat), F32),
            sds((held_chunks, half_rows, feat), BF16),
        ),
        [pltpu.VMEM((chunks, half_rows, feat), F32)],
        1,
        2,
        cols * feat,
    )(place, keep, other)
    passed = stepped(pass_on, *steps[0])
    share_rows = half_rows // reps
    dealt = held_chunks * share_rows
    mine, *parts = call(
        deal_kernel,
        (sds((dealt, feat), F32), *[sds((dealt + feat, row_count), BF16)] * 3),
        [pltpu.VMEM((held_chunks, half_rows, feat), F32)],
        1,
        5,
        cols * feat,
    )(place, stay, passed, far1, far2, far3)
    parts = [shifted(part, k + 1) for k, part in enumerate(parts)]
    query_grad_t = own_t
    for part in parts:
        mine = mine + part[:dealt].astype(F32)
        query_grad_t = query_grad_t + part[dealt:].astype(F32)
    for axis, partner in steps[1:]:
        half = mine.shape[0] // 2
        more = stepped(mine[half:].astype(BF16), axis, partner)
        mine = mine[:half] + more.astype(F32)
    codebook_grad = mine

    directory = arrived[:, 0, held : held + pair_count].astype(jnp.int32)
    local_iota = jnp.arange(PBLK_DEV, dtype=jnp.int32)
    named = jnp.any(
        directory[:, :, None] == here_blk * PBLK_DEV + local_iota[None, None, :], axis=1
    )
    slot_j = []
    for k in range(CAP):
        rank = jnp.zeros((owners,), jnp.int32)
        found = jnp.full((owners,), PBLK_DEV, jnp.int32)
        for j in range(PBLK_DEV):
            found = jnp.where(named[:, j] & (rank == k), j, found)
            rank = rank + named[:, j].astype(jnp.int32)
        slot_j.append(found)
    slot_j = jnp.stack(slot_j, axis=1).reshape(-1)
    passage_grad = call(
        return_kernel,
        sds((PBLK_DEV * PR, feat), F32),
        [pltpu.VMEM((PBLK_DEV + 1, PR, feat), F32) for _ in range(4)],
        1,
        3,
        owners * CAP * PR * feat,
    )(slot_j, returned, unit, inverse_wide)
    return (
        loss[None],
        query_grad_t.T[None, None],
        passage_grad[None, None],
        codebook_grad,
    )


def solution(mesh):
    reps = mesh.shape["rep"]
    torus = Mesh(mesh.devices.reshape(4, -1, 2, reps), AXES)
    in_specs = (
        P(BLK, "rep", None, None),
        P(BLK, None, None),
        P(BLK, None),
        P(BLK, "rep", None, None),
        P(),
    )
    out_specs = (
        P(BLK, "rep", None),
        P(BLK, "rep", None, None),
        P(BLK, "rep", None, None),
        P(AXES, None),
    )
    return jax.shard_map(
        shards, mesh=torus, in_specs=in_specs, out_specs=out_specs, check_vma=False
    )
```

```python
import functools

import jax
import jax.numpy as jnp
from jax import lax
from jax.experimental import pallas as pl
from jax.experimental.pallas import tpu as pltpu
from jax.sharding import Mesh
from jax.sharding import PartitionSpec as P


CODES = 256
BOOKS = 8
PR = 16
PBLK_DEV = 4
CAP = 2
LANES = 128
AXES = ("x", "z", "c", "rep")
BLK = ("x", "z", "c")
EPS = 1e-06
INTERPRET = False
VMEM_LIMIT = 10 << 20
WHOLE_VMEM = 63_000_000

F32 = jnp.float32
BF16 = jnp.bfloat16
VMEM = pl.BlockSpec(memory_space=pltpu.VMEM)
SMEM = pl.BlockSpec(memory_space=pltpu.SMEM)
HBM = pl.BlockSpec(memory_space=pltpu.HBM)
CONTRACT_LAST = (((1,), (1,)), ((), ()))
CONTRACT_FIRST = (((0,), (0,)), ((), ()))


def call(kernel, out_shape, scratch, smem_count, vmem_count, flops, hbm_count=0,
         limit=VMEM_LIMIT):
    out_bytes = sum(s.size * s.dtype.itemsize for s in jax.tree.leaves(out_shape))
    return pl.pallas_call(
        kernel,
        out_shape=out_shape,
        in_specs=[SMEM] * smem_count + [HBM] * hbm_count + [VMEM] * vmem_count,
        out_specs=jax.tree.map(lambda _: VMEM, out_shape),
        scratch_shapes=scratch,
        interpret=INTERPRET,
        compiler_params=pltpu.CompilerParams(vmem_limit_bytes=limit),
        cost_estimate=pl.CostEstimate(
            flops=flops, bytes_accessed=2 * out_bytes, transcendentals=0
        ),
    )


def sds(shape, dtype):
    return jax.ShapeDtypeStruct(shape, dtype)


def one_hot_of(codes_ref, book, rows):
    cols = codes_ref.shape[1]
    row = codes_ref[book : book + 1, :]
    iota = lax.broadcasted_iota(jnp.int32, (rows, cols), 0).astype(F32)
    return jnp.where(row == iota, 1.0, 0.0).astype(BF16)


def fill_keys(pair_s, key_ref, pair_count):
    sub = lax.broadcasted_iota(jnp.int32, (PR, LANES), 0)
    for slot in range(pair_count):
        key_ref[slot * PR : (slot + 1) * PR, :] = sub + pair_s[0, slot] * PR


def hits(key_ref, start, count, tkey_ref):
    keys = key_ref[start : start + count, :]
    width = tkey_ref.shape[1]
    wide = jnp.concatenate([keys] * (width // LANES), axis=1)
    return wide == tkey_ref[...]


def stats_kernel(
    pair_s, place_s, recv_ref, near_ref, far_ref, tkey_ref, cbt_ref,
    u_ref, q_ref, st_ref, codes_ref, unit_ref, inv_ref, rows_ref, key_ref,
):
    cols = u_ref.shape[0]
    pair_count = cols // PR
    rep = place_s[3]
    rows = near_ref.shape[0] // 2
    across = q_ref.shape[0] // rows - 1 - rep
    for owner, part in (
        (rep, near_ref[0:rows, :]),
        (rep ^ 1, near_ref[rows : 2 * rows, :]),
        (across, far_ref[0:rows, :]),
        (across ^ 1, far_ref[rows : 2 * rows, :]),
    ):
        q_ref[pl.ds(pl.multiple_of(owner * rows, rows), rows), :] = part
    rows_ref[...] = recv_ref[...].astype(F32)
    lane_group = lax.broadcasted_iota(jnp.int32, (BOOKS, LANES), 1) // PR
    per_tile = LANES // PR
    for tile in range(cols // LANES):
        held = jnp.zeros((BOOKS, LANES), F32)
        for place in range(per_tile):
            block = pair_s[0, tile * per_tile + place]
            owner = block >> 2
            within = block & 3
            codes = rows_ref[pl.ds(pl.multiple_of(owner * BOOKS, BOOKS), BOOKS), :]
            turned = pltpu.roll(codes, lax.rem(LANES + (place - within) * PR, LANES), axis=1)
            held = jnp.where(lane_group == place, turned, held)
        codes_ref[:, tile * LANES : (tile + 1) * LANES] = held
    fill_keys(pair_s, key_ref, pair_count)
    quant = jnp.zeros((cbt_ref.shape[0], cols), F32)
    for book in range(BOOKS):
        quant = quant + jnp.dot(
            cbt_ref[:, book * CODES : (book + 1) * CODES],
            one_hot_of(codes_ref, book, CODES),
            preferred_element_type=F32,
        )
    inverse = lax.rsqrt(jnp.sum(quant * quant, axis=0, keepdims=True) + EPS)
    unit = quant * inverse
    unit_ref[...] = unit
    inv_ref[...] = inverse
    u_ref[...] = unit.T.astype(BF16)
    total_rows = q_ref.shape[0]
    peak = jnp.full((1, total_rows), -1e30, F32)
    total = jnp.zeros((1, total_rows), F32)
    hit = jnp.zeros((1, total_rows), F32)
    step = min(256, cols)
    for start in range(0, cols, step):
        scores = lax.dot_general(
            u_ref[start : start + step, :], q_ref[...], CONTRACT_LAST, preferred_element_type=F32
        )
        fresh = jnp.maximum(peak, jnp.max(scores, axis=0, keepdims=True))
        total = total * jnp.exp(peak - fresh) + jnp.sum(
            jnp.exp(scores - fresh), axis=0, keepdims=True
        )
        peak = fresh
        hit = hit + jnp.sum(
            jnp.where(hits(key_ref, start, step, tkey_ref), scores, 0.0), axis=0, keepdims=True
        )
    st_ref[0:1, :] = peak
    st_ref[1:2, :] = total
    st_ref[2:3, :] = hit


def hot_kernel(codes_ref, u_ref, q_ref, st_ref, hot_ref, exp_ref):
    for book in range(BOOKS):
        hot_ref[book] = one_hot_of(codes_ref, book, CODES)
    cols = u_ref.shape[0]
    step = min(256, cols)
    for start in range(0, cols, step):
        span = slice(start, start + step)
        scores = lax.dot_general(
            u_ref[span, :], q_ref[...], CONTRACT_LAST, preferred_element_type=F32
        )
        exp_ref[span, :] = jnp.exp(scores - st_ref[0:1, :])


def pack_kernel(codes_hbm, pairs_hbm, out_ref, codes_ref, pairs_ref, sems):
    copies = [
        pltpu.make_async_copy(codes_hbm, codes_ref, sems.at[0]),
        pltpu.make_async_copy(pairs_hbm, pairs_ref, sems.at[1]),
    ]
    for copy in copies:
        copy.start()
    for copy in copies:
        copy.wait()
    codes = codes_ref[...]
    spare = LANES - codes.shape[1] - pairs_ref.shape[1]
    pieces = [codes, jnp.broadcast_to(pairs_ref[...], (BOOKS, pairs_ref.shape[1]))]
    if spare:
        pieces.append(jnp.zeros((BOOKS, spare), jnp.int32))
    message = jnp.concatenate(pieces, axis=1).astype(F32).astype(BF16)
    for peer in range(out_ref.shape[0]):
        out_ref[peer] = message


def side_kernel(
    place_s, codes_hbm, pairs_hbm, targets_hbm, books_hbm,
    pairs_ref, slot_ref, tkey_ref, cbt_ref, unit_ref,
    codes_ref, near_ref, targets_ref, books_ref, float_ref, sems,
):
    moves = (
        (codes_hbm, codes_ref),
        (pairs_hbm, near_ref),
        (targets_hbm, targets_ref),
        (books_hbm, books_ref),
    )
    copies = [pltpu.make_async_copy(a, b, sems.at[k]) for k, (a, b) in enumerate(moves)]
    for copy in copies:
        copy.start()
    for copy in copies:
        copy.wait()
    rep = place_s[3]
    pairs_ref[...] = near_ref[...]
    count = near_ref.shape[1]
    wide = jnp.broadcast_to(near_ref[...], (count, count))
    tall = wide.astype(F32).T.astype(jnp.int32)
    before = ((tall >> 2) == (wide >> 2)) & (tall < wide)
    slot_ref[...] = (near_ref[...] >> 2) * CAP + jnp.sum(
        jnp.where(before, 1, 0), axis=0, keepdims=True
    )
    reps, rows = targets_ref.shape
    for k in range(reps):
        target = targets_ref[k : k + 1, :]
        block = target // (PR * reps)
        within = target - block * (PR * reps)
        mine = within // PR == rep
        tkey_ref[:, k * rows : (k + 1) * rows] = jnp.where(
            mine, block * PR + within - rep * PR, -1
        )
    float_ref[...] = codes_ref[...].astype(F32)
    quant = jnp.zeros((unit_ref.shape[0], cbt_ref.shape[0]), F32)
    for book in range(BOOKS):
        span = slice(book * CODES, (book + 1) * CODES)
        words = books_ref[span, :]
        cbt_ref[:, span] = words.T
        quant = quant + lax.dot_general(
            one_hot_of(float_ref, book, CODES), words, CONTRACT_FIRST, preferred_element_type=F32
        )
    inverse = lax.rsqrt(jnp.sum(quant * quant, axis=1, keepdims=True) + EPS)
    feat = quant.shape[1]
    unit_ref[:, 0:feat] = quant * inverse
    unit_ref[:, feat:] = jnp.broadcast_to(inverse, (quant.shape[0], LANES))


def merged(first, second):
    peak = jnp.maximum(first[0:1], second[0:1])
    total = first[1:2] * jnp.exp(first[0:1] - peak) + second[1:2] * jnp.exp(second[0:1] - peak)
    return peak, total, first[2:3] + second[2:3]


def grads_kernel(
    pair_s, slot_s, place_s,
    st_ref, sta_ref, stb_ref, tkey_ref, u_ref, q_ref, unit_ref, inv_ref, hot_ref, exp_ref,
    send_ref, loss_ref, own_ref, far_ref, stay_ref, give_ref,
    key_ref, lse_ref, qgt_ref, pg_ref, sum_ref, *, sizes,
):
    cols = u_ref.shape[0]
    pair_count = cols // PR
    x_here, z_here, rep = place_s[0], place_s[1], place_s[3]
    x_count, z_count = sizes
    rows = own_ref.shape[1]
    peak, total, hit = merged(sta_ref[...], stb_ref[...])
    lse = peak + jnp.log(total)
    factor = jnp.exp(st_ref[0:1, :] - lse)
    lse_ref[0:1, :] = lse - hit
    loss_ref[...] = lse_ref[0:1, pl.ds(pl.multiple_of(rep * rows, rows), rows)]
    fill_keys(pair_s, key_ref, pair_count)
    send_ref[...] = jnp.zeros(send_ref.shape, BF16)
    step = min(256, cols)
    grown = None
    for start in range(0, cols, step):
        span = slice(start, start + step)
        u_part = u_ref[span, :]
        hit_mask = hits(key_ref, start, step, tkey_ref)
        weight = (exp_ref[span, :] * factor - jnp.where(hit_mask, 1.0, 0.0)).astype(BF16)
        grad = jnp.dot(weight, q_ref[...], preferred_element_type=F32)
        narrow = grad.astype(BF16)
        for place in range(step // PR):
            send_ref[slot_s[0, start // PR + place]] = narrow[place * PR : (place + 1) * PR, :]
        turned = grad.T
        unit = unit_ref[:, span]
        along = jnp.sum(unit * turned, axis=0, keepdims=True)
        pg_ref[:, span] = (inv_ref[0:1, span] * (turned - unit * along)).astype(BF16)
        term = lax.dot_general(u_part, weight, CONTRACT_FIRST, preferred_element_type=F32)
        grown = term if grown is None else grown + term
    qgt_ref[...] = grown
    count = q_ref.shape[0] // rows
    for k in range(count):
        owner = lax.rem(rep + k, count)
        part = qgt_ref[:, pl.ds(pl.multiple_of(owner * rows, rows), rows)]
        if k:
            far_ref[k - 1] = part.astype(BF16)
        else:
            own_ref[...] = part
    for book in range(BOOKS):
        sum_ref[book * CODES : (book + 1) * CODES, :] = lax.dot_general(
            hot_ref[book], pg_ref[...], CONTRACT_LAST, preferred_element_type=F32
        )
    half = z_count // 2
    size = stay_ref.shape[1]
    z_order = halving_order(z_here, z_partners(z_count))
    for at, px in enumerate(halving_order(x_here, x_partners(x_count))):
        for k in range(half):
            near = pl.multiple_of((px * z_count + z_order[k]) * size, size)
            there = pl.multiple_of((px * z_count + z_order[half + k]) * size, size)
            stay_ref[at * half + k] = sum_ref[pl.ds(near, size), :]
            give_ref[at * half + k] = sum_ref[pl.ds(there, size), :].astype(BF16)


def x_partners(count):
    if count == 4:
        return [lambda i: i ^ 1, lambda i: 3 - i]
    return [lambda i: i ^ 1][: count - 1]


def z_partners(count):
    if count == 8:
        return [
            lambda i: i ^ 1,
            lambda i: (i - 1 + 2 * (i & 1)) & 7,
            lambda i: (i + 3 - 6 * (i & 1)) & 7,
        ]
    return [lambda i: i ^ 1][: count - 1]


def halving_order(here, partners):
    order = [here]
    for partner in reversed(partners):
        order = order + halving_tail(partner(here), partners, len(order))
    return order


def halving_tail(there, partners, length):
    order = [there]
    for partner in reversed(partners):
        if len(order) == length:
            break
        order = order + halving_tail(partner(there), partners, len(order))
    return order


def split_kernel(place_s, stay_ref, recv_ref, keep_ref, give_ref, sum_ref):
    core = place_s[2]
    half = keep_ref.shape[1]
    sum_ref[...] = stay_ref[...] + recv_ref[...].astype(F32)
    mine = pl.ds(pl.multiple_of(core * half, half), half)
    other = pl.ds(pl.multiple_of((1 - core) * half, half), half)
    for chunk in range(keep_ref.shape[0]):
        keep_ref[chunk] = sum_ref[chunk, mine, :]
        give_ref[chunk] = sum_ref[chunk, other, :].astype(BF16)


def deal_kernel(place_s, stay_ref, recv_ref, qg_ref, own_ref, far1, far2, far3, sum_ref):
    rep = place_s[3]
    chunks = stay_ref.shape[0]
    share = own_ref.shape[0] // chunks
    reps = stay_ref.shape[1] // share
    sum_ref[...] = stay_ref[...] + recv_ref[...].astype(F32)
    for k, out in enumerate((own_ref, far1, far2, far3)):
        owner = lax.rem(rep + k, reps)
        at = pl.ds(pl.multiple_of(owner * share, share), share)
        for pair in range(chunks // 2):
            rows = jnp.concatenate(
                [sum_ref[2 * pair, at, :], sum_ref[2 * pair + 1, at, :]], axis=0
            )
            out[2 * pair * share : (2 * pair + 2) * share, :] = rows.astype(out.dtype)
    dealt = own_ref.shape[0]
    for k, out in enumerate((far1, far2, far3)):
        out[dealt:, :] = qg_ref[k]


def return_kernel(slot_j, ret_ref, unit_ref, out_ref, *sums):
    for part in sums:
        part[...] = jnp.zeros(part.shape, F32)
    for slot in range(ret_ref.shape[0]):
        part = sums[slot % len(sums)]
        j = slot_j[slot]
        part[j] = part[j] + ret_ref[slot].astype(F32)
    for j in range(PBLK_DEV):
        grad = sums[0][j]
        for part in sums[1:]:
            grad = grad + part[j]
        feat = out_ref.shape[1]
        unit = unit_ref[j * PR : (j + 1) * PR, 0:feat]
        inverse = unit_ref[j * PR : (j + 1) * PR, feat : feat + 1]
        out_ref[j * PR : (j + 1) * PR, :] = inverse * (
            grad - unit * jnp.sum(unit * grad, axis=1, keepdims=True)
        )


def shifted(x, k):
    count = lax.axis_size("rep")
    return lax.ppermute(x, "rep", [(i, (i + k) % count) for i in range(count)])


def stepped(x, axis, partner):
    return lax.ppermute(x, axis, [(i, partner(i)) for i in range(lax.axis_size(axis))])


def shards(query_embed, positive_ids, pair_blocks, code_ids, codebooks):
    reps = lax.axis_size("rep")
    x_count, z_count, cores = (lax.axis_size(a) for a in BLK)
    owners = x_count * z_count * cores
    here_blk = lax.axis_index(BLK)
    rows_mine = query_embed[0, 0]
    row_count, feat = rows_mine.shape
    all_rows = reps * row_count
    wanted = pair_blocks[0]
    pair_count = wanted.shape[0]
    cols = pair_count * PR
    local_codes = code_ids[0, 0]
    place = jnp.stack([lax.axis_index(a) for a in AXES]).astype(jnp.int32)
    near = [(i, i ^ 1) for i in range(reps)]
    cross = [(i, reps - 1 - i) for i in range(reps)]
    pairs_in = wanted[None, :]
    held = local_codes.shape[1]

    rows_near = lax.ppermute(rows_mine, "rep", near)
    message = call(
        pack_kernel,
        sds((owners, BOOKS, LANES), BF16),
        [
            pltpu.VMEM((BOOKS, held), jnp.int32),
            pltpu.VMEM((1, pair_count), jnp.int32),
            pltpu.SemaphoreType.DMA((2,)),
        ],
        0,
        0,
        owners * BOOKS * LANES,
        2,
        WHOLE_VMEM,
    )(local_codes, pairs_in)
    arrived = lax.all_to_all(message, BLK, 0, 0, tiled=True)
    rows_pair = jnp.concatenate([rows_mine, rows_near], axis=0)
    rows_far = lax.ppermute(rows_pair, "rep", cross)
    pairs, slot_of, tkey, turned_books, unit = call(
        side_kernel,
        (
            sds((1, pair_count), jnp.int32),
            sds((1, pair_count), jnp.int32),
            sds((1, all_rows), jnp.int32),
            sds((feat, BOOKS * CODES), BF16),
            sds((held, feat + LANES), F32),
        ),
        [
            pltpu.VMEM((BOOKS, held), jnp.int32),
            pltpu.VMEM((1, pair_count), jnp.int32),
            pltpu.VMEM((reps, row_count), jnp.int32),
            pltpu.VMEM((BOOKS * CODES, feat), BF16),
            pltpu.VMEM((BOOKS, held), F32),
            pltpu.SemaphoreType.DMA((4,)),
        ],
        1,
        0,
        2 * BOOKS * CODES * feat * held,
        4,
    )(place, local_codes, pairs_in, positive_ids[0], codebooks)

    units, queries, stats, codes, unit_t, inv_t = call(
        stats_kernel,
        (
            sds((cols, feat), BF16),
            sds((all_rows, feat), BF16),
            sds((3, all_rows), F32),
            sds((BOOKS, cols), F32),
            sds((feat, cols), F32),
            sds((1, cols), F32),
        ),
        [pltpu.VMEM((owners * BOOKS, LANES), F32), pltpu.VMEM((cols, LANES), jnp.int32)],
        2,
        5,
        2 * cols * feat * (BOOKS * CODES + all_rows),
    )(
        pairs, place, arrived.reshape(owners * BOOKS, LANES),
        rows_pair, rows_far, tkey, turned_books,
    )

    stats_near = lax.ppermute(stats, "rep", near)
    hot, powers = call(
        hot_kernel,
        (sds((BOOKS, CODES, cols), BF16), sds((cols, all_rows), F32)),
        [],
        0,
        4,
        BOOKS * CODES * cols,
    )(codes, units, queries, stats)
    stats_two = jnp.concatenate(merged(stats, stats_near), axis=0)
    stats_far = lax.ppermute(stats_two, "rep", cross)

    chunks = x_count * z_count
    chunk_rows = codebooks.shape[0] // chunks
    half_rows = chunk_rows // cores
    held_chunks = chunks // 2
    outbound, loss, own_t, far, stay, give = call(
        functools.partial(grads_kernel, sizes=(x_count, z_count)),
        (
            sds((owners * CAP, PR, feat), BF16),
            sds((1, row_count), F32),
            sds((feat, row_count), F32),
            sds((reps - 1, feat, row_count), BF16),
            sds((held_chunks, chunk_rows, feat), F32),
            sds((held_chunks, chunk_rows, feat), BF16),
        ),
        [
            pltpu.VMEM((cols, LANES), jnp.int32),
            pltpu.VMEM((8, all_rows), F32),
            pltpu.VMEM((feat, all_rows), F32),
            pltpu.VMEM((feat, cols), BF16),
            pltpu.VMEM((BOOKS * CODES, feat), F32),
        ],
        3,
        10,
        cols * feat * (4 * all_rows + 2 * BOOKS * CODES),
    )(
        pairs, slot_of, place,
        stats, stats_two, stats_far, tkey, units, queries, unit_t, inv_t, hot, powers,
    )

    outbound = outbound.reshape(owners, CAP * PR, feat)
    returned = lax.all_to_all(outbound, BLK, 0, 0, tiled=True)
    returned = returned.reshape(owners * CAP, PR, feat)

    steps = [("z", partner) for partner in z_partners(z_count)]
    steps = steps[:1] + [("x", partner) for partner in x_partners(x_count)] + steps[1:]
    passed = stepped(give, *steps[0])
    keep, hand = call(
        split_kernel,
        (
            sds((held_chunks, half_rows, feat), F32),
            sds((held_chunks, half_rows, feat), BF16),
        ),
        [pltpu.VMEM((held_chunks, chunk_rows, feat), F32)],
        1,
        2,
        cols * feat,
    )(place, stay, passed)
    other = lax.ppermute(hand, "c", [(0, 1), (1, 0)])
    share_rows = half_rows // reps
    dealt = held_chunks * share_rows
    mine, *parts = call(
        deal_kernel,
        (sds((dealt, feat), F32), *[sds((dealt + feat, row_count), BF16)] * 3),
        [pltpu.VMEM((held_chunks, half_rows, feat), F32)],
        1,
        3,
        cols * feat,
    )(place, keep, other, far)
    parts = [shifted(part, k + 1) for k, part in enumerate(parts)]
    query_grad_t = own_t
    for part in parts:
        mine = mine + part[:dealt].astype(F32)
        query_grad_t = query_grad_t + part[dealt:].astype(F32)
    for axis, partner in steps[1:]:
        half = mine.shape[0] // 2
        more = stepped(mine[half:].astype(BF16), axis, partner)
        mine = mine[:half] + more.astype(F32)
    codebook_grad = mine

    directory = arrived[:, 0, held : held + pair_count].astype(jnp.int32)
    local_iota = jnp.arange(PBLK_DEV, dtype=jnp.int32)
    named = jnp.any(
        directory[:, :, None] == here_blk * PBLK_DEV + local_iota[None, None, :], axis=1
    )
    slot_j = []
    for k in range(CAP):
        rank = jnp.zeros((owners,), jnp.int32)
        found = jnp.full((owners,), PBLK_DEV, jnp.int32)
        for j in range(PBLK_DEV):
            found = jnp.where(named[:, j] & (rank == k), j, found)
            rank = rank + named[:, j].astype(jnp.int32)
        slot_j.append(found)
    slot_j = jnp.stack(slot_j, axis=1).reshape(-1)
    passage_grad = call(
        return_kernel,
        sds((PBLK_DEV * PR, feat), F32),
        [pltpu.VMEM((PBLK_DEV + 1, PR, feat), F32) for _ in range(4)],
        1,
        2,
        owners * CAP * PR * feat,
    )(slot_j, returned, unit)
    return (
        loss[None],
        query_grad_t.T[None, None],
        passage_grad[None, None],
        codebook_grad,
    )


def solution(mesh):
    reps = mesh.shape["rep"]
    torus = Mesh(mesh.devices.reshape(4, -1, 2, reps), AXES)
    in_specs = (
        P(BLK, "rep", None, None),
        P(BLK, None, None),
        P(BLK, None),
        P(BLK, "rep", None, None),
        P(),
    )
    out_specs = (
        P(BLK, "rep", None),
        P(BLK, "rep", None, None),
        P(BLK, "rep", None, None),
        P(AXES, None),
    )
    return jax.shard_map(
        shards, mesh=torus, in_specs=in_specs, out_specs=out_specs, check_vma=False
    )
```

```python
import functools

import jax
import jax.numpy as jnp
from jax import lax
from jax.experimental import pallas as pl
from jax.experimental.pallas import tpu as pltpu
from jax.sharding import Mesh
from jax.sharding import PartitionSpec as P


CODES = 256
BOOKS = 8
PR = 16
PBLK_DEV = 4
CAP = 2
LANES = 128
AXES = ("x", "z", "c", "rep")
BLK = ("x", "z", "c")
EPS = 1e-06
INTERPRET = False
VMEM_LIMIT = 10 << 20
WHOLE_VMEM = 63_000_000

F32 = jnp.float32
BF16 = jnp.bfloat16
VMEM = pl.BlockSpec(memory_space=pltpu.VMEM)
SMEM = pl.BlockSpec(memory_space=pltpu.SMEM)
HBM = pl.BlockSpec(memory_space=pltpu.HBM)
CONTRACT_LAST = (((1,), (1,)), ((), ()))
CONTRACT_FIRST = (((0,), (0,)), ((), ()))


def call(kernel, out_shape, scratch, smem_count, vmem_count, flops, hbm_count=0,
         limit=VMEM_LIMIT):
    out_bytes = sum(s.size * s.dtype.itemsize for s in jax.tree.leaves(out_shape))
    return pl.pallas_call(
        kernel,
        out_shape=out_shape,
        in_specs=[SMEM] * smem_count + [HBM] * hbm_count + [VMEM] * vmem_count,
        out_specs=jax.tree.map(lambda _: VMEM, out_shape),
        scratch_shapes=scratch,
        interpret=INTERPRET,
        compiler_params=pltpu.CompilerParams(vmem_limit_bytes=limit),
        cost_estimate=pl.CostEstimate(
            flops=flops, bytes_accessed=2 * out_bytes, transcendentals=0
        ),
    )


def sds(shape, dtype):
    return jax.ShapeDtypeStruct(shape, dtype)


def one_hot_of(codes_ref, book, rows):
    cols = codes_ref.shape[1]
    row = codes_ref[book : book + 1, :]
    iota = lax.broadcasted_iota(jnp.int32, (rows, cols), 0).astype(F32)
    return jnp.where(row == iota, 1.0, 0.0).astype(BF16)


def fill_keys(pair_s, key_ref, pair_count):
    sub = lax.broadcasted_iota(jnp.int32, (PR, LANES), 0)
    for slot in range(pair_count):
        key_ref[slot * PR : (slot + 1) * PR, :] = sub + pair_s[0, slot] * PR


def hits(key_ref, start, count, tkey_ref):
    keys = key_ref[start : start + count, :]
    width = tkey_ref.shape[1]
    wide = jnp.concatenate([keys] * (width // LANES), axis=1)
    return wide == tkey_ref[...]


def stats_kernel(
    pair_s, place_s, recv_ref, near_ref, far_ref, tkey_ref, cbt_ref,
    u_ref, q_ref, st_ref, codes_ref, unit_ref, inv_ref, rows_ref, key_ref,
):
    cols = u_ref.shape[0]
    pair_count = cols // PR
    rep = place_s[3]
    rows = near_ref.shape[0] // 2
    across = q_ref.shape[0] // rows - 1 - rep
    for owner, part in (
        (rep, near_ref[0:rows, :]),
        (rep ^ 1, near_ref[rows : 2 * rows, :]),
        (across, far_ref[0:rows, :]),
        (across ^ 1, far_ref[rows : 2 * rows, :]),
    ):
        q_ref[pl.ds(pl.multiple_of(owner * rows, rows), rows), :] = part
    rows_ref[...] = recv_ref[...].astype(F32)
    lane_group = lax.broadcasted_iota(jnp.int32, (BOOKS, LANES), 1) // PR
    per_tile = LANES // PR
    for tile in range(cols // LANES):
        held = jnp.zeros((BOOKS, LANES), F32)
        for place in range(per_tile):
            block = pair_s[0, tile * per_tile + place]
            owner = block >> 2
            within = block & 3
            codes = rows_ref[pl.ds(pl.multiple_of(owner * BOOKS, BOOKS), BOOKS), :]
            turned = pltpu.roll(codes, lax.rem(LANES + (place - within) * PR, LANES), axis=1)
            held = jnp.where(lane_group == place, turned, held)
        codes_ref[:, tile * LANES : (tile + 1) * LANES] = held
    fill_keys(pair_s, key_ref, pair_count)
    quant = jnp.zeros((cbt_ref.shape[0], cols), F32)
    for book in range(BOOKS):
        quant = quant + jnp.dot(
            cbt_ref[:, book * CODES : (book + 1) * CODES],
            one_hot_of(codes_ref, book, CODES),
            preferred_element_type=F32,
        )
    inverse = lax.rsqrt(jnp.sum(quant * quant, axis=0, keepdims=True) + EPS)
    unit = quant * inverse
    unit_ref[...] = unit
    inv_ref[...] = inverse
    u_ref[...] = unit.T.astype(BF16)
    total_rows = q_ref.shape[0]
    peak = jnp.full((1, total_rows), -1e30, F32)
    total = jnp.zeros((1, total_rows), F32)
    hit = jnp.zeros((1, total_rows), F32)
    step = min(256, cols)
    for start in range(0, cols, step):
        scores = lax.dot_general(
            u_ref[start : start + step, :], q_ref[...], CONTRACT_LAST, preferred_element_type=F32
        )
        fresh = jnp.maximum(peak, jnp.max(scores, axis=0, keepdims=True))
        total = total * jnp.exp(peak - fresh) + jnp.sum(
            jnp.exp(scores - fresh), axis=0, keepdims=True
        )
        peak = fresh
        hit = hit + jnp.sum(
            jnp.where(hits(key_ref, start, step, tkey_ref), scores, 0.0), axis=0, keepdims=True
        )
    st_ref[0:1, :] = peak
    st_ref[1:2, :] = total
    st_ref[2:3, :] = hit


def hot_kernel(codes_ref, u_ref, q_ref, st_ref, hot_ref, exp_ref):
    for book in range(BOOKS):
        hot_ref[book] = one_hot_of(codes_ref, book, CODES)
    cols = u_ref.shape[0]
    step = min(256, cols)
    for start in range(0, cols, step):
        span = slice(start, start + step)
        scores = lax.dot_general(
            u_ref[span, :], q_ref[...], CONTRACT_LAST, preferred_element_type=F32
        )
        exp_ref[span, :] = jnp.exp(scores - st_ref[0:1, :])


def pack_kernel(codes_hbm, pairs_hbm, out_ref, codes_ref, pairs_ref, sems):
    copies = [
        pltpu.make_async_copy(codes_hbm, codes_ref, sems.at[0]),
        pltpu.make_async_copy(pairs_hbm, pairs_ref, sems.at[1]),
    ]
    for copy in copies:
        copy.start()
    for copy in copies:
        copy.wait()
    codes = codes_ref[...]
    spare = LANES - codes.shape[1] - pairs_ref.shape[1]
    pieces = [codes, jnp.broadcast_to(pairs_ref[...], (BOOKS, pairs_ref.shape[1]))]
    if spare:
        pieces.append(jnp.zeros((BOOKS, spare), jnp.int32))
    message = jnp.concatenate(pieces, axis=1).astype(F32).astype(BF16)
    for peer in range(out_ref.shape[0]):
        out_ref[peer] = message


def side_kernel(
    place_s, codes_hbm, pairs_hbm, targets_hbm, books_hbm,
    pairs_ref, slot_ref, tkey_ref, cbt_ref, unit_ref,
    codes_ref, near_ref, targets_ref, books_ref, float_ref, sems,
):
    moves = (
        (codes_hbm, codes_ref),
        (pairs_hbm, near_ref),
        (targets_hbm, targets_ref),
        (books_hbm, books_ref),
    )
    copies = [pltpu.make_async_copy(a, b, sems.at[k]) for k, (a, b) in enumerate(moves)]
    for copy in copies:
        copy.start()
    for copy in copies:
        copy.wait()
    rep = place_s[3]
    pairs_ref[...] = near_ref[...]
    count = near_ref.shape[1]
    wide = jnp.broadcast_to(near_ref[...], (count, count))
    tall = wide.astype(F32).T.astype(jnp.int32)
    before = ((tall >> 2) == (wide >> 2)) & (tall < wide)
    slot_ref[...] = (near_ref[...] >> 2) * CAP + jnp.sum(
        jnp.where(before, 1, 0), axis=0, keepdims=True
    )
    reps, rows = targets_ref.shape
    for k in range(reps):
        target = targets_ref[k : k + 1, :]
        block = target // (PR * reps)
        within = target - block * (PR * reps)
        mine = within // PR == rep
        tkey_ref[:, k * rows : (k + 1) * rows] = jnp.where(
            mine, block * PR + within - rep * PR, -1
        )
    float_ref[...] = codes_ref[...].astype(F32)
    quant = jnp.zeros((unit_ref.shape[0], cbt_ref.shape[0]), F32)
    for book in range(BOOKS):
        span = slice(book * CODES, (book + 1) * CODES)
        words = books_ref[span, :]
        cbt_ref[:, span] = words.T
        quant = quant + lax.dot_general(
            one_hot_of(float_ref, book, CODES), words, CONTRACT_FIRST, preferred_element_type=F32
        )
    inverse = lax.rsqrt(jnp.sum(quant * quant, axis=1, keepdims=True) + EPS)
    feat = quant.shape[1]
    unit_ref[:, 0:feat] = quant * inverse
    unit_ref[:, feat:] = jnp.broadcast_to(inverse, (quant.shape[0], LANES))


def merged(first, second):
    peak = jnp.maximum(first[0:1], second[0:1])
    total = first[1:2] * jnp.exp(first[0:1] - peak) + second[1:2] * jnp.exp(second[0:1] - peak)
    return peak, total, first[2:3] + second[2:3]


def grads_kernel(
    pair_s, slot_s, place_s,
    st_ref, sta_ref, stb_ref, tkey_ref, u_ref, q_ref, unit_ref, inv_ref, hot_ref, exp_ref,
    send_ref, loss_ref, held_ref, lent_ref, stay_ref, give_ref,
    key_ref, lse_ref, qgt_ref, pg_ref, sum_ref, *, sizes,
):
    cols = u_ref.shape[0]
    pair_count = cols // PR
    x_here, z_here, rep = place_s[0], place_s[1], place_s[3]
    x_count, z_count = sizes
    rows = held_ref.shape[2]
    peak, total, hit = merged(sta_ref[...], stb_ref[...])
    lse = peak + jnp.log(total)
    factor = jnp.exp(st_ref[0:1, :] - lse)
    lse_ref[0:1, :] = lse - hit
    loss_ref[...] = lse_ref[0:1, pl.ds(pl.multiple_of(rep * rows, rows), rows)]
    fill_keys(pair_s, key_ref, pair_count)
    send_ref[...] = jnp.zeros(send_ref.shape, BF16)
    step = min(256, cols)
    grown = None
    for start in range(0, cols, step):
        span = slice(start, start + step)
        u_part = u_ref[span, :]
        hit_mask = hits(key_ref, start, step, tkey_ref)
        weight = (exp_ref[span, :] * factor - jnp.where(hit_mask, 1.0, 0.0)).astype(BF16)
        grad = jnp.dot(weight, q_ref[...], preferred_element_type=F32)
        narrow = grad.astype(BF16)
        for place in range(step // PR):
            send_ref[slot_s[0, start // PR + place]] = narrow[place * PR : (place + 1) * PR, :]
        turned = grad.T
        unit = unit_ref[:, span]
        along = jnp.sum(unit * turned, axis=0, keepdims=True)
        pg_ref[:, span] = (inv_ref[0:1, span] * (turned - unit * along)).astype(BF16)
        term = lax.dot_general(u_part, weight, CONTRACT_FIRST, preferred_element_type=F32)
        grown = term if grown is None else grown + term
    qgt_ref[...] = grown
    count = q_ref.shape[0] // rows
    for out, first in ((held_ref, rep), (lent_ref, rep ^ 1)):
        for k, owner in enumerate((first, count - 1 - first)):
            part = qgt_ref[:, pl.ds(pl.multiple_of(owner * rows, rows), rows)]
            out[k] = part.astype(out.dtype)
    for book in range(BOOKS):
        sum_ref[book * CODES : (book + 1) * CODES, :] = lax.dot_general(
            hot_ref[book], pg_ref[...], CONTRACT_LAST, preferred_element_type=F32
        )
    half = z_count // 2
    size = stay_ref.shape[1]
    z_order = halving_order(z_here, z_partners(z_count))
    for at, px in enumerate(halving_order(x_here, x_partners(x_count))):
        for k in range(half):
            near = pl.multiple_of((px * z_count + z_order[k]) * size, size)
            there = pl.multiple_of((px * z_count + z_order[half + k]) * size, size)
            stay_ref[at * half + k] = sum_ref[pl.ds(near, size), :]
            give_ref[at * half + k] = sum_ref[pl.ds(there, size), :].astype(BF16)


def x_partners(count):
    if count == 4:
        return [lambda i: i ^ 1, lambda i: 3 - i]
    return [lambda i: i ^ 1][: count - 1]


def z_partners(count):
    if count == 8:
        return [
            lambda i: i ^ 1,
            lambda i: (i - 1 + 2 * (i & 1)) & 7,
            lambda i: (i + 3 - 6 * (i & 1)) & 7,
        ]
    return [lambda i: i ^ 1][: count - 1]


def halving_order(here, partners):
    order = [here]
    for partner in reversed(partners):
        order = order + halving_tail(partner(here), partners, len(order))
    return order


def halving_tail(there, partners, length):
    order = [there]
    for partner in reversed(partners):
        if len(order) == length:
            break
        order = order + halving_tail(partner(there), partners, len(order))
    return order


def split_kernel(
    place_s, stay_ref, recv_ref, held_ref, back_ref, keep_ref, give_ref, own_ref, far_ref, sum_ref
):
    own_ref[...] = held_ref[0] + back_ref[0].astype(F32)
    far_ref[...] = (held_ref[1] + back_ref[1].astype(F32)).astype(BF16)
    core = place_s[2]
    half = keep_ref.shape[1]
    sum_ref[...] = stay_ref[...] + recv_ref[...].astype(F32)
    mine = pl.ds(pl.multiple_of(core * half, half), half)
    other = pl.ds(pl.multiple_of((1 - core) * half, half), half)
    for chunk in range(keep_ref.shape[0]):
        keep_ref[chunk] = sum_ref[chunk, mine, :]
        give_ref[chunk] = sum_ref[chunk, other, :].astype(BF16)


def deal_kernel(place_s, stay_ref, recv_ref, own_ref, far1, far2, far3, sum_ref):
    rep = place_s[3]
    chunks = stay_ref.shape[0]
    share = own_ref.shape[0] // chunks
    reps = stay_ref.shape[1] // share
    sum_ref[...] = stay_ref[...] + recv_ref[...].astype(F32)
    for k, out in enumerate((own_ref, far1, far2, far3)):
        owner = lax.rem(rep + k, reps)
        at = pl.ds(pl.multiple_of(owner * share, share), share)
        for pair in range(chunks // 2):
            rows = jnp.concatenate(
                [sum_ref[2 * pair, at, :], sum_ref[2 * pair + 1, at, :]], axis=0
            )
            out[2 * pair * share : (2 * pair + 2) * share, :] = rows.astype(out.dtype)


def last_kernel(own_ref, far_ref, out_ref):
    out_ref[...] = (own_ref[...] + far_ref[...].astype(F32)).T


def return_kernel(slot_j, ret_ref, unit_ref, out_ref, *sums):
    for part in sums:
        part[...] = jnp.zeros(part.shape, F32)
    for slot in range(ret_ref.shape[0]):
        part = sums[slot % len(sums)]
        j = slot_j[slot]
        part[j] = part[j] + ret_ref[slot].astype(F32)
    for j in range(PBLK_DEV):
        grad = sums[0][j]
        for part in sums[1:]:
            grad = grad + part[j]
        feat = out_ref.shape[1]
        unit = unit_ref[j * PR : (j + 1) * PR, 0:feat]
        inverse = unit_ref[j * PR : (j + 1) * PR, feat : feat + 1]
        out_ref[j * PR : (j + 1) * PR, :] = inverse * (
            grad - unit * jnp.sum(unit * grad, axis=1, keepdims=True)
        )


def shifted(x, k):
    count = lax.axis_size("rep")
    return lax.ppermute(x, "rep", [(i, (i + k) % count) for i in range(count)])


def stepped(x, axis, partner):
    return lax.ppermute(x, axis, [(i, partner(i)) for i in range(lax.axis_size(axis))])


def shards(query_embed, positive_ids, pair_blocks, code_ids, codebooks):
    reps = lax.axis_size("rep")
    x_count, z_count, cores = (lax.axis_size(a) for a in BLK)
    owners = x_count * z_count * cores
    here_blk = lax.axis_index(BLK)
    rows_mine = query_embed[0, 0]
    row_count, feat = rows_mine.shape
    all_rows = reps * row_count
    wanted = pair_blocks[0]
    pair_count = wanted.shape[0]
    cols = pair_count * PR
    local_codes = code_ids[0, 0]
    place = jnp.stack([lax.axis_index(a) for a in AXES]).astype(jnp.int32)
    near = [(i, i ^ 1) for i in range(reps)]
    cross = [(i, reps - 1 - i) for i in range(reps)]
    pairs_in = wanted[None, :]
    held = local_codes.shape[1]

    rows_near = lax.ppermute(rows_mine, "rep", near)
    message = call(
        pack_kernel,
        sds((owners, BOOKS, LANES), BF16),
        [
            pltpu.VMEM((BOOKS, held), jnp.int32),
            pltpu.VMEM((1, pair_count), jnp.int32),
            pltpu.SemaphoreType.DMA((2,)),
        ],
        0,
        0,
        owners * BOOKS * LANES,
        2,
        WHOLE_VMEM,
    )(local_codes, pairs_in)
    arrived = lax.all_to_all(message, BLK, 0, 0, tiled=True)
    rows_pair = jnp.concatenate([rows_mine, rows_near], axis=0)
    rows_far = lax.ppermute(rows_pair, "rep", cross)
    pairs, slot_of, tkey, turned_books, unit = call(
        side_kernel,
        (
            sds((1, pair_count), jnp.int32),
            sds((1, pair_count), jnp.int32),
            sds((1, all_rows), jnp.int32),
            sds((feat, BOOKS * CODES), BF16),
            sds((held, feat + LANES), F32),
        ),
        [
            pltpu.VMEM((BOOKS, held), jnp.int32),
            pltpu.VMEM((1, pair_count), jnp.int32),
            pltpu.VMEM((reps, row_count), jnp.int32),
            pltpu.VMEM((BOOKS * CODES, feat), BF16),
            pltpu.VMEM((BOOKS, held), F32),
            pltpu.SemaphoreType.DMA((4,)),
        ],
        1,
        0,
        2 * BOOKS * CODES * feat * held,
        4,
    )(place, local_codes, pairs_in, positive_ids[0], codebooks)

    units, queries, stats, codes, unit_t, inv_t = call(
        stats_kernel,
        (
            sds((cols, feat), BF16),
            sds((all_rows, feat), BF16),
            sds((3, all_rows), F32),
            sds((BOOKS, cols), F32),
            sds((feat, cols), F32),
            sds((1, cols), F32),
        ),
        [pltpu.VMEM((owners * BOOKS, LANES), F32), pltpu.VMEM((cols, LANES), jnp.int32)],
        2,
        5,
        2 * cols * feat * (BOOKS * CODES + all_rows),
    )(
        pairs, place, arrived.reshape(owners * BOOKS, LANES),
        rows_pair, rows_far, tkey, turned_books,
    )

    stats_near = lax.ppermute(stats, "rep", near)
    hot, powers = call(
        hot_kernel,
        (sds((BOOKS, CODES, cols), BF16), sds((cols, all_rows), F32)),
        [],
        0,
        4,
        BOOKS * CODES * cols,
    )(codes, units, queries, stats)
    stats_two = jnp.concatenate(merged(stats, stats_near), axis=0)
    stats_far = lax.ppermute(stats_two, "rep", cross)

    chunks = x_count * z_count
    chunk_rows = codebooks.shape[0] // chunks
    half_rows = chunk_rows // cores
    held_chunks = chunks // 2
    outbound, loss, held_t, lent_t, stay, give = call(
        functools.partial(grads_kernel, sizes=(x_count, z_count)),
        (
            sds((owners * CAP, PR, feat), BF16),
            sds((1, row_count), F32),
            sds((2, feat, row_count), F32),
            sds((2, feat, row_count), BF16),
            sds((held_chunks, chunk_rows, feat), F32),
            sds((held_chunks, chunk_rows, feat), BF16),
        ),
        [
            pltpu.VMEM((cols, LANES), jnp.int32),
            pltpu.VMEM((8, all_rows), F32),
            pltpu.VMEM((feat, all_rows), F32),
            pltpu.VMEM((feat, cols), BF16),
            pltpu.VMEM((BOOKS * CODES, feat), F32),
        ],
        3,
        10,
        cols * feat * (4 * all_rows + 2 * BOOKS * CODES),
    )(
        pairs, slot_of, place,
        stats, stats_two, stats_far, tkey, units, queries, unit_t, inv_t, hot, powers,
    )

    outbound = outbound.reshape(owners, CAP * PR, feat)
    returned = lax.all_to_all(outbound, BLK, 0, 0, tiled=True)
    returned = returned.reshape(owners * CAP, PR, feat)

    steps = [("z", partner) for partner in z_partners(z_count)]
    steps = steps[:1] + [("x", partner) for partner in x_partners(x_count)] + steps[1:]
    passed = stepped(give, *steps[0])
    lent_back = lax.ppermute(lent_t, "rep", near)
    keep, hand, own_t, far_t = call(
        split_kernel,
        (
            sds((held_chunks, half_rows, feat), F32),
            sds((held_chunks, half_rows, feat), BF16),
            sds((feat, row_count), F32),
            sds((feat, row_count), BF16),
        ),
        [pltpu.VMEM((held_chunks, chunk_rows, feat), F32)],
        1,
        4,
        cols * feat,
    )(place, stay, passed, held_t, lent_back)
    other = lax.ppermute(hand, "c", [(0, 1), (1, 0)])
    far_t = lax.ppermute(far_t, "rep", cross)
    share_rows = half_rows // reps
    dealt = held_chunks * share_rows
    mine, *parts = call(
        deal_kernel,
        (sds((dealt, feat), F32), *[sds((dealt, feat), BF16)] * 3),
        [pltpu.VMEM((held_chunks, half_rows, feat), F32)],
        1,
        2,
        cols * feat,
    )(place, keep, other)
    parts = [shifted(part, k + 1) for k, part in enumerate(parts)]
    for part in parts:
        mine = mine + part.astype(F32)
    query_grad = call(
        last_kernel, sds((row_count, feat), F32), [], 0, 2, row_count * feat
    )(own_t, far_t)
    for axis, partner in steps[1:]:
        half = mine.shape[0] // 2
        more = stepped(mine[half:].astype(BF16), axis, partner)
        mine = mine[:half] + more.astype(F32)
    codebook_grad = mine

    directory = arrived[:, 0, held : held + pair_count].astype(jnp.int32)
    local_iota = jnp.arange(PBLK_DEV, dtype=jnp.int32)
    named = jnp.any(
        directory[:, :, None] == here_blk * PBLK_DEV + local_iota[None, None, :], axis=1
    )
    slot_j = []
    for k in range(CAP):
        rank = jnp.zeros((owners,), jnp.int32)
        found = jnp.full((owners,), PBLK_DEV, jnp.int32)
        for j in range(PBLK_DEV):
            found = jnp.where(named[:, j] & (rank == k), j, found)
            rank = rank + named[:, j].astype(jnp.int32)
        slot_j.append(found)
    slot_j = jnp.stack(slot_j, axis=1).reshape(-1)
    passage_grad = call(
        return_kernel,
        sds((PBLK_DEV * PR, feat), F32),
        [pltpu.VMEM((PBLK_DEV + 1, PR, feat), F32) for _ in range(4)],
        1,
        2,
        owners * CAP * PR * feat,
    )(slot_j, returned, unit)
    return (
        loss[None],
        query_grad[None, None],
        passage_grad[None, None],
        codebook_grad,
    )


def solution(mesh):
    reps = mesh.shape["rep"]
    torus = Mesh(mesh.devices.reshape(4, -1, 2, reps), AXES)
    in_specs = (
        P(BLK, "rep", None, None),
        P(BLK, None, None),
        P(BLK, None),
        P(BLK, "rep", None, None),
        P(),
    )
    out_specs = (
        P(BLK, "rep", None),
        P(BLK, "rep", None, None),
        P(BLK, "rep", None, None),
        P(AXES, None),
    )
    return jax.shard_map(
        shards, mesh=torus, in_specs=in_specs, out_specs=out_specs, check_vma=False
    )
```

```python
import functools

import jax
import jax.numpy as jnp
from jax import lax
from jax.experimental import pallas as pl
from jax.experimental.pallas import tpu as pltpu
from jax.sharding import Mesh
from jax.sharding import PartitionSpec as P


CODES = 256
BOOKS = 8
PR = 16
PBLK_DEV = 4
CAP = 2
LANES = 128
AXES = ("x", "z", "c", "rep")
BLK = ("x", "z", "c")
EPS = 1e-06
INTERPRET = False
VMEM_LIMIT = 10 << 20
WHOLE_VMEM = 63_000_000

F32 = jnp.float32
BF16 = jnp.bfloat16
VMEM = pl.BlockSpec(memory_space=pltpu.VMEM)
SMEM = pl.BlockSpec(memory_space=pltpu.SMEM)
HBM = pl.BlockSpec(memory_space=pltpu.HBM)
CONTRACT_LAST = (((1,), (1,)), ((), ()))
CONTRACT_FIRST = (((0,), (0,)), ((), ()))


def call(kernel, out_shape, scratch, smem_count, vmem_count, flops, hbm_count=0,
         limit=VMEM_LIMIT):
    out_bytes = sum(s.size * s.dtype.itemsize for s in jax.tree.leaves(out_shape))
    return pl.pallas_call(
        kernel,
        out_shape=out_shape,
        in_specs=[SMEM] * smem_count + [HBM] * hbm_count + [VMEM] * vmem_count,
        out_specs=jax.tree.map(lambda _: VMEM, out_shape),
        scratch_shapes=scratch,
        interpret=INTERPRET,
        compiler_params=pltpu.CompilerParams(vmem_limit_bytes=limit),
        cost_estimate=pl.CostEstimate(
            flops=flops, bytes_accessed=2 * out_bytes, transcendentals=0
        ),
    )


def sds(shape, dtype):
    return jax.ShapeDtypeStruct(shape, dtype)


def one_hot_of(codes_ref, book, rows):
    cols = codes_ref.shape[1]
    row = codes_ref[book : book + 1, :]
    iota = lax.broadcasted_iota(jnp.int32, (rows, cols), 0).astype(F32)
    return jnp.where(row == iota, 1.0, 0.0).astype(BF16)


def fill_keys(pair_s, key_ref, pair_count):
    sub = lax.broadcasted_iota(jnp.int32, (PR, LANES), 0)
    for slot in range(pair_count):
        key_ref[slot * PR : (slot + 1) * PR, :] = sub + pair_s[0, slot] * PR


def hits(key_ref, start, count, tkey_ref):
    keys = key_ref[start : start + count, :]
    width = tkey_ref.shape[1]
    wide = jnp.concatenate([keys] * (width // LANES), axis=1)
    return wide == tkey_ref[...]


def stats_kernel(
    pair_s, place_s, recv_ref, near_ref, far_ref, tkey_ref, cbt_ref,
    u_ref, q_ref, st_ref, codes_ref, unit_ref, inv_ref, rows_ref, key_ref,
):
    cols = u_ref.shape[0]
    pair_count = cols // PR
    rep = place_s[3]
    rows = near_ref.shape[0] // 2
    across = q_ref.shape[0] // rows - 1 - rep
    for owner, part in (
        (rep, near_ref[0:rows, :]),
        (rep ^ 1, near_ref[rows : 2 * rows, :]),
        (across, far_ref[0:rows, :]),
        (across ^ 1, far_ref[rows : 2 * rows, :]),
    ):
        q_ref[pl.ds(pl.multiple_of(owner * rows, rows), rows), :] = part
    rows_ref[...] = recv_ref[...].astype(F32)
    lane_group = lax.broadcasted_iota(jnp.int32, (BOOKS, LANES), 1) // PR
    per_tile = LANES // PR
    for tile in range(cols // LANES):
        held = jnp.zeros((BOOKS, LANES), F32)
        for place in range(per_tile):
            block = pair_s[0, tile * per_tile + place]
            owner = block >> 2
            within = block & 3
            codes = rows_ref[pl.ds(pl.multiple_of(owner * BOOKS, BOOKS), BOOKS), :]
            turned = pltpu.roll(codes, lax.rem(LANES + (place - within) * PR, LANES), axis=1)
            held = jnp.where(lane_group == place, turned, held)
        codes_ref[:, tile * LANES : (tile + 1) * LANES] = held
    fill_keys(pair_s, key_ref, pair_count)
    quant = jnp.zeros((cbt_ref.shape[0], cols), F32)
    for book in range(BOOKS):
        quant = quant + jnp.dot(
            cbt_ref[:, book * CODES : (book + 1) * CODES],
            one_hot_of(codes_ref, book, CODES),
            preferred_element_type=F32,
        )
    inverse = lax.rsqrt(jnp.sum(quant * quant, axis=0, keepdims=True) + EPS)
    unit = quant * inverse
    unit_ref[...] = unit
    inv_ref[...] = inverse
    u_ref[...] = unit.T.astype(BF16)
    total_rows = q_ref.shape[0]
    peak = jnp.full((1, total_rows), -1e30, F32)
    total = jnp.zeros((1, total_rows), F32)
    hit = jnp.zeros((1, total_rows), F32)
    step = min(256, cols)
    for start in range(0, cols, step):
        scores = lax.dot_general(
            u_ref[start : start + step, :], q_ref[...], CONTRACT_LAST, preferred_element_type=F32
        )
        fresh = jnp.maximum(peak, jnp.max(scores, axis=0, keepdims=True))
        total = total * jnp.exp(peak - fresh) + jnp.sum(
            jnp.exp(scores - fresh), axis=0, keepdims=True
        )
        peak = fresh
        hit = hit + jnp.sum(
            jnp.where(hits(key_ref, start, step, tkey_ref), scores, 0.0), axis=0, keepdims=True
        )
    st_ref[0:1, :] = peak
    st_ref[1:2, :] = total
    st_ref[2:3, :] = hit


def hot_kernel(codes_ref, u_ref, q_ref, st_ref, hot_ref, exp_ref):
    for book in range(BOOKS):
        hot_ref[book] = one_hot_of(codes_ref, book, CODES)
    cols = u_ref.shape[0]
    step = min(256, cols)
    for start in range(0, cols, step):
        span = slice(start, start + step)
        scores = lax.dot_general(
            u_ref[span, :], q_ref[...], CONTRACT_LAST, preferred_element_type=F32
        )
        exp_ref[span, :] = jnp.exp(scores - st_ref[0:1, :])


def pack_kernel(codes_hbm, pairs_hbm, out_ref, codes_ref, pairs_ref, sems):
    copies = [
        pltpu.make_async_copy(codes_hbm, codes_ref, sems.at[0]),
        pltpu.make_async_copy(pairs_hbm, pairs_ref, sems.at[1]),
    ]
    for copy in copies:
        copy.start()
    for copy in copies:
        copy.wait()
    codes = codes_ref[...]
    spare = LANES - codes.shape[1] - pairs_ref.shape[1]
    pieces = [codes, jnp.broadcast_to(pairs_ref[...], (BOOKS, pairs_ref.shape[1]))]
    if spare:
        pieces.append(jnp.zeros((BOOKS, spare), jnp.int32))
    message = jnp.concatenate(pieces, axis=1).astype(F32).astype(BF16)
    for peer in range(out_ref.shape[0]):
        out_ref[peer] = message


def side_kernel(
    place_s, codes_hbm, pairs_hbm, targets_hbm, books_hbm,
    pairs_ref, slot_ref, tkey_ref, cbt_ref, unit_ref,
    codes_ref, near_ref, targets_ref, books_ref, float_ref, sems,
):
    moves = (
        (codes_hbm, codes_ref),
        (pairs_hbm, near_ref),
        (targets_hbm, targets_ref),
        (books_hbm, books_ref),
    )
    copies = [pltpu.make_async_copy(a, b, sems.at[k]) for k, (a, b) in enumerate(moves)]
    for copy in copies:
        copy.start()
    for copy in copies:
        copy.wait()
    rep = place_s[3]
    pairs_ref[...] = near_ref[...]
    count = near_ref.shape[1]
    wide = jnp.broadcast_to(near_ref[...], (count, count))
    tall = wide.astype(F32).T.astype(jnp.int32)
    before = ((tall >> 2) == (wide >> 2)) & (tall < wide)
    slot_ref[...] = (near_ref[...] >> 2) * CAP + jnp.sum(
        jnp.where(before, 1, 0), axis=0, keepdims=True
    )
    reps, rows = targets_ref.shape
    for k in range(reps):
        target = targets_ref[k : k + 1, :]
        block = target // (PR * reps)
        within = target - block * (PR * reps)
        mine = within // PR == rep
        tkey_ref[:, k * rows : (k + 1) * rows] = jnp.where(
            mine, block * PR + within - rep * PR, -1
        )
    float_ref[...] = codes_ref[...].astype(F32)
    quant = jnp.zeros((unit_ref.shape[0], cbt_ref.shape[0]), F32)
    for book in range(BOOKS):
        span = slice(book * CODES, (book + 1) * CODES)
        words = books_ref[span, :]
        cbt_ref[:, span] = words.T
        quant = quant + lax.dot_general(
            one_hot_of(float_ref, book, CODES), words, CONTRACT_FIRST, preferred_element_type=F32
        )
    inverse = lax.rsqrt(jnp.sum(quant * quant, axis=1, keepdims=True) + EPS)
    feat = quant.shape[1]
    unit_ref[:, 0:feat] = quant * inverse
    unit_ref[:, feat:] = jnp.broadcast_to(inverse, (quant.shape[0], LANES))


def merged(first, second):
    peak = jnp.maximum(first[0:1], second[0:1])
    total = first[1:2] * jnp.exp(first[0:1] - peak) + second[1:2] * jnp.exp(second[0:1] - peak)
    return peak, total, first[2:3] + second[2:3]


def grads_kernel(
    pair_s, slot_s, place_s,
    st_ref, sta_ref, stb_ref, tkey_ref, u_ref, q_ref, unit_ref, inv_ref, hot_ref, exp_ref,
    send_ref, loss_ref, held_ref, lent_ref, stay_ref, give_ref,
    key_ref, lse_ref, qgt_ref, pg_ref, sum_ref, *, sizes,
):
    cols = u_ref.shape[0]
    pair_count = cols // PR
    x_here, z_here, rep = place_s[0], place_s[1], place_s[3]
    x_count, z_count = sizes
    rows = held_ref.shape[2]
    peak, total, hit = merged(sta_ref[...], stb_ref[...])
    lse = peak + jnp.log(total)
    factor = jnp.exp(st_ref[0:1, :] - lse)
    lse_ref[0:1, :] = lse - hit
    loss_ref[...] = lse_ref[0:1, pl.ds(pl.multiple_of(rep * rows, rows), rows)]
    fill_keys(pair_s, key_ref, pair_count)
    send_ref[...] = jnp.zeros(send_ref.shape, BF16)
    step = min(256, cols)
    grown = None
    for start in range(0, cols, step):
        span = slice(start, start + step)
        u_part = u_ref[span, :]
        hit_mask = hits(key_ref, start, step, tkey_ref)
        weight = (exp_ref[span, :] * factor - jnp.where(hit_mask, 1.0, 0.0)).astype(BF16)
        grad = jnp.dot(weight, q_ref[...], preferred_element_type=F32)
        narrow = grad.astype(BF16)
        for place in range(step // PR):
            send_ref[slot_s[0, start // PR + place]] = narrow[place * PR : (place + 1) * PR, :]
        turned = grad.T
        unit = unit_ref[:, span]
        along = jnp.sum(unit * turned, axis=0, keepdims=True)
        pg_ref[:, span] = (inv_ref[0:1, span] * (turned - unit * along)).astype(BF16)
        term = lax.dot_general(u_part, weight, CONTRACT_FIRST, preferred_element_type=F32)
        grown = term if grown is None else grown + term
    qgt_ref[...] = grown
    count = q_ref.shape[0] // rows
    for out, first in ((held_ref, rep), (lent_ref, rep ^ 1)):
        for k, owner in enumerate((first, count - 1 - first)):
            part = qgt_ref[:, pl.ds(pl.multiple_of(owner * rows, rows), rows)]
            out[k] = part.astype(out.dtype)
    for book in range(BOOKS):
        sum_ref[book * CODES : (book + 1) * CODES, :] = lax.dot_general(
            hot_ref[book], pg_ref[...], CONTRACT_LAST, preferred_element_type=F32
        )
    half = z_count // 2
    size = stay_ref.shape[1]
    z_order = halving_order(z_here, z_partners(z_count))
    for at, px in enumerate(halving_order(x_here, x_partners(x_count))):
        for k in range(half):
            near = pl.multiple_of((px * z_count + z_order[k]) * size, size)
            there = pl.multiple_of((px * z_count + z_order[half + k]) * size, size)
            stay_ref[at * half + k] = sum_ref[pl.ds(near, size), :]
            give_ref[at * half + k] = sum_ref[pl.ds(there, size), :].astype(BF16)


def x_partners(count):
    if count == 4:
        return [lambda i: i ^ 1, lambda i: 3 - i]
    return [lambda i: i ^ 1][: count - 1]


def z_partners(count):
    if count == 8:
        return [
            lambda i: i ^ 1,
            lambda i: (i - 1 + 2 * (i & 1)) & 7,
            lambda i: (i + 3 - 6 * (i & 1)) & 7,
        ]
    return [lambda i: i ^ 1][: count - 1]


def halving_order(here, partners):
    order = [here]
    for partner in reversed(partners):
        order = order + halving_tail(partner(here), partners, len(order))
    return order


def halving_tail(there, partners, length):
    order = [there]
    for partner in reversed(partners):
        if len(order) == length:
            break
        order = order + halving_tail(partner(there), partners, len(order))
    return order


def split_kernel(place_s, stay_ref, recv_ref, keep_ref, give_ref, sum_ref):
    core = place_s[2]
    half = keep_ref.shape[1]
    sum_ref[...] = stay_ref[...] + recv_ref[...].astype(F32)
    mine = pl.ds(pl.multiple_of(core * half, half), half)
    other = pl.ds(pl.multiple_of((1 - core) * half, half), half)
    for chunk in range(keep_ref.shape[0]):
        keep_ref[chunk] = sum_ref[chunk, mine, :]
        give_ref[chunk] = sum_ref[chunk, other, :].astype(BF16)


def deal_kernel(
    place_s, stay_ref, recv_ref, held_ref, back_ref,
    own_ref, far1, far2, far3, half_ref, over_ref, sum_ref,
):
    half_ref[...] = held_ref[0] + back_ref[0].astype(F32)
    over_ref[...] = (held_ref[1] + back_ref[1].astype(F32)).astype(BF16)
    rep = place_s[3]
    chunks = stay_ref.shape[0]
    share = own_ref.shape[0] // chunks
    reps = stay_ref.shape[1] // share
    sum_ref[...] = stay_ref[...] + recv_ref[...].astype(F32)
    for k, out in enumerate((own_ref, far1, far2, far3)):
        owner = lax.rem(rep + k, reps)
        at = pl.ds(pl.multiple_of(owner * share, share), share)
        for pair in range(chunks // 2):
            rows = jnp.concatenate(
                [sum_ref[2 * pair, at, :], sum_ref[2 * pair + 1, at, :]], axis=0
            )
            out[2 * pair * share : (2 * pair + 2) * share, :] = rows.astype(out.dtype)


def last_kernel(own_ref, far_ref, out_ref):
    out_ref[...] = (own_ref[...] + far_ref[...].astype(F32)).T


def return_kernel(slot_j, ret_ref, unit_ref, out_ref, *sums):
    for part in sums:
        part[...] = jnp.zeros(part.shape, F32)
    for slot in range(ret_ref.shape[0]):
        part = sums[slot % len(sums)]
        j = slot_j[slot]
        part[j] = part[j] + ret_ref[slot].astype(F32)
    for j in range(PBLK_DEV):
        grad = sums[0][j]
        for part in sums[1:]:
            grad = grad + part[j]
        feat = out_ref.shape[1]
        unit = unit_ref[j * PR : (j + 1) * PR, 0:feat]
        inverse = unit_ref[j * PR : (j + 1) * PR, feat : feat + 1]
        out_ref[j * PR : (j + 1) * PR, :] = inverse * (
            grad - unit * jnp.sum(unit * grad, axis=1, keepdims=True)
        )


def shifted(x, k):
    count = lax.axis_size("rep")
    return lax.ppermute(x, "rep", [(i, (i + k) % count) for i in range(count)])


def stepped(x, axis, partner):
    return lax.ppermute(x, axis, [(i, partner(i)) for i in range(lax.axis_size(axis))])


def shards(query_embed, positive_ids, pair_blocks, code_ids, codebooks):
    reps = lax.axis_size("rep")
    x_count, z_count, cores = (lax.axis_size(a) for a in BLK)
    owners = x_count * z_count * cores
    here_blk = lax.axis_index(BLK)
    rows_mine = query_embed[0, 0]
    row_count, feat = rows_mine.shape
    all_rows = reps * row_count
    wanted = pair_blocks[0]
    pair_count = wanted.shape[0]
    cols = pair_count * PR
    local_codes = code_ids[0, 0]
    place = jnp.stack([lax.axis_index(a) for a in AXES]).astype(jnp.int32)
    near = [(i, i ^ 1) for i in range(reps)]
    cross = [(i, reps - 1 - i) for i in range(reps)]
    pairs_in = wanted[None, :]
    held = local_codes.shape[1]

    rows_near = lax.ppermute(rows_mine, "rep", near)
    message = call(
        pack_kernel,
        sds((owners, BOOKS, LANES), BF16),
        [
            pltpu.VMEM((BOOKS, held), jnp.int32),
            pltpu.VMEM((1, pair_count), jnp.int32),
            pltpu.SemaphoreType.DMA((2,)),
        ],
        0,
        0,
        owners * BOOKS * LANES,
        2,
        WHOLE_VMEM,
    )(local_codes, pairs_in)
    arrived = lax.all_to_all(message, BLK, 0, 0, tiled=True)
    rows_pair = jnp.concatenate([rows_mine, rows_near], axis=0)
    rows_far = lax.ppermute(rows_pair, "rep", cross)
    pairs, slot_of, tkey, turned_books, unit = call(
        side_kernel,
        (
            sds((1, pair_count), jnp.int32),
            sds((1, pair_count), jnp.int32),
            sds((1, all_rows), jnp.int32),
            sds((feat, BOOKS * CODES), BF16),
            sds((held, feat + LANES), F32),
        ),
        [
            pltpu.VMEM((BOOKS, held), jnp.int32),
            pltpu.VMEM((1, pair_count), jnp.int32),
            pltpu.VMEM((reps, row_count), jnp.int32),
            pltpu.VMEM((BOOKS * CODES, feat), BF16),
            pltpu.VMEM((BOOKS, held), F32),
            pltpu.SemaphoreType.DMA((4,)),
        ],
        1,
        0,
        2 * BOOKS * CODES * feat * held,
        4,
    )(place, local_codes, pairs_in, positive_ids[0], codebooks)

    units, queries, stats, codes, unit_t, inv_t = call(
        stats_kernel,
        (
            sds((cols, feat), BF16),
            sds((all_rows, feat), BF16),
            sds((3, all_rows), F32),
            sds((BOOKS, cols), F32),
            sds((feat, cols), F32),
            sds((1, cols), F32),
        ),
        [pltpu.VMEM((owners * BOOKS, LANES), F32), pltpu.VMEM((cols, LANES), jnp.int32)],
        2,
        5,
        2 * cols * feat * (BOOKS * CODES + all_rows),
    )(
        pairs, place, arrived.reshape(owners * BOOKS, LANES),
        rows_pair, rows_far, tkey, turned_books,
    )

    stats_near = lax.ppermute(stats, "rep", near)
    hot, powers = call(
        hot_kernel,
        (sds((BOOKS, CODES, cols), BF16), sds((cols, all_rows), F32)),
        [],
        0,
        4,
        BOOKS * CODES * cols,
    )(codes, units, queries, stats)
    stats_two = jnp.concatenate(merged(stats, stats_near), axis=0)
    stats_far = lax.ppermute(stats_two, "rep", cross)

    chunks = x_count * z_count
    chunk_rows = codebooks.shape[0] // chunks
    half_rows = chunk_rows // cores
    held_chunks = chunks // 2
    outbound, loss, held_t, lent_t, stay, give = call(
        functools.partial(grads_kernel, sizes=(x_count, z_count)),
        (
            sds((owners * CAP, PR, feat), BF16),
            sds((1, row_count), F32),
            sds((2, feat, row_count), F32),
            sds((2, feat, row_count), BF16),
            sds((held_chunks, chunk_rows, feat), F32),
            sds((held_chunks, chunk_rows, feat), BF16),
        ),
        [
            pltpu.VMEM((cols, LANES), jnp.int32),
            pltpu.VMEM((8, all_rows), F32),
            pltpu.VMEM((feat, all_rows), F32),
            pltpu.VMEM((feat, cols), BF16),
            pltpu.VMEM((BOOKS * CODES, feat), F32),
        ],
        3,
        10,
        cols * feat * (4 * all_rows + 2 * BOOKS * CODES),
    )(
        pairs, slot_of, place,
        stats, stats_two, stats_far, tkey, units, queries, unit_t, inv_t, hot, powers,
    )

    outbound = outbound.reshape(owners, CAP * PR, feat)
    returned = lax.all_to_all(outbound, BLK, 0, 0, tiled=True)
    returned = returned.reshape(owners * CAP, PR, feat)

    steps = [("z", partner) for partner in z_partners(z_count)]
    steps = steps[:1] + [("x", partner) for partner in x_partners(x_count)] + steps[1:]
    passed = stepped(give, *steps[0])
    lent_back = lax.ppermute(lent_t, "rep", near)
    keep, hand = call(
        split_kernel,
        (
            sds((held_chunks, half_rows, feat), F32),
            sds((held_chunks, half_rows, feat), BF16),
        ),
        [pltpu.VMEM((held_chunks, chunk_rows, feat), F32)],
        1,
        2,
        cols * feat,
    )(place, stay, passed)
    other = lax.ppermute(hand, "c", [(0, 1), (1, 0)])
    share_rows = half_rows // reps
    dealt = held_chunks * share_rows
    mine, *parts, own_t, far_t = call(
        deal_kernel,
        (
            sds((dealt, feat), F32),
            *[sds((dealt, feat), BF16)] * 3,
            sds((feat, row_count), F32),
            sds((feat, row_count), BF16),
        ),
        [pltpu.VMEM((held_chunks, half_rows, feat), F32)],
        1,
        4,
        cols * feat,
    )(place, keep, other, held_t, lent_back)
    far_t = lax.ppermute(far_t, "rep", cross)
    parts = [shifted(part, k + 1) for k, part in enumerate(parts)]
    for part in parts:
        mine = mine + part.astype(F32)
    query_grad = call(
        last_kernel, sds((row_count, feat), F32), [], 0, 2, row_count * feat
    )(own_t, far_t)
    for axis, partner in steps[1:]:
        half = mine.shape[0] // 2
        more = stepped(mine[half:].astype(BF16), axis, partner)
        mine = mine[:half] + more.astype(F32)
    codebook_grad = mine

    directory = arrived[:, 0, held : held + pair_count].astype(jnp.int32)
    local_iota = jnp.arange(PBLK_DEV, dtype=jnp.int32)
    named = jnp.any(
        directory[:, :, None] == here_blk * PBLK_DEV + local_iota[None, None, :], axis=1
    )
    slot_j = []
    for k in range(CAP):
        rank = jnp.zeros((owners,), jnp.int32)
        found = jnp.full((owners,), PBLK_DEV, jnp.int32)
        for j in range(PBLK_DEV):
            found = jnp.where(named[:, j] & (rank == k), j, found)
            rank = rank + named[:, j].astype(jnp.int32)
        slot_j.append(found)
    slot_j = jnp.stack(slot_j, axis=1).reshape(-1)
    passage_grad = call(
        return_kernel,
        sds((PBLK_DEV * PR, feat), F32),
        [pltpu.VMEM((PBLK_DEV + 1, PR, feat), F32) for _ in range(4)],
        1,
        2,
        owners * CAP * PR * feat,
    )(slot_j, returned, unit)
    return (
        loss[None],
        query_grad[None, None],
        passage_grad[None, None],
        codebook_grad,
    )


def solution(mesh):
    reps = mesh.shape["rep"]
    torus = Mesh(mesh.devices.reshape(4, -1, 2, reps), AXES)
    in_specs = (
        P(BLK, "rep", None, None),
        P(BLK, None, None),
        P(BLK, None),
        P(BLK, "rep", None, None),
        P(),
    )
    out_specs = (
        P(BLK, "rep", None),
        P(BLK, "rep", None, None),
        P(BLK, "rep", None, None),
        P(AXES, None),
    )
    return jax.shard_map(
        shards, mesh=torus, in_specs=in_specs, out_specs=out_specs, check_vma=False
    )
```

```python
import functools

import jax
import jax.numpy as jnp
from jax import lax
from jax.experimental import pallas as pl
from jax.experimental.pallas import tpu as pltpu
from jax.sharding import Mesh
from jax.sharding import PartitionSpec as P


CODES = 256
BOOKS = 8
PR = 16
PBLK_DEV = 4
CAP = 2
LANES = 128
AXES = ("x", "z", "c", "rep")
BLK = ("x", "z", "c")
EPS = 1e-06
INTERPRET = False
VMEM_LIMIT = 10 << 20
WHOLE_VMEM = 63_000_000

F32 = jnp.float32
BF16 = jnp.bfloat16
VMEM = pl.BlockSpec(memory_space=pltpu.VMEM)
SMEM = pl.BlockSpec(memory_space=pltpu.SMEM)
HBM = pl.BlockSpec(memory_space=pltpu.HBM)
CONTRACT_LAST = (((1,), (1,)), ((), ()))
CONTRACT_FIRST = (((0,), (0,)), ((), ()))


def call(kernel, out_shape, scratch, smem_count, vmem_count, flops, hbm_count=0,
         limit=VMEM_LIMIT):
    out_bytes = sum(s.size * s.dtype.itemsize for s in jax.tree.leaves(out_shape))
    return pl.pallas_call(
        kernel,
        out_shape=out_shape,
        in_specs=[SMEM] * smem_count + [HBM] * hbm_count + [VMEM] * vmem_count,
        out_specs=jax.tree.map(lambda _: VMEM, out_shape),
        scratch_shapes=scratch,
        interpret=INTERPRET,
        compiler_params=pltpu.CompilerParams(vmem_limit_bytes=limit),
        cost_estimate=pl.CostEstimate(
            flops=flops, bytes_accessed=2 * out_bytes, transcendentals=0
        ),
    )


def sds(shape, dtype):
    return jax.ShapeDtypeStruct(shape, dtype)


def one_hot_of(codes_ref, book, rows):
    cols = codes_ref.shape[1]
    row = codes_ref[book : book + 1, :]
    iota = lax.broadcasted_iota(jnp.int32, (rows, cols), 0).astype(F32)
    return jnp.where(row == iota, 1.0, 0.0).astype(BF16)


def fill_keys(pair_s, key_ref, pair_count):
    sub = lax.broadcasted_iota(jnp.int32, (PR, LANES), 0)
    for slot in range(pair_count):
        key_ref[slot * PR : (slot + 1) * PR, :] = sub + pair_s[0, slot] * PR


def hits(key_ref, start, count, tkey_ref):
    keys = key_ref[start : start + count, :]
    width = tkey_ref.shape[1]
    wide = jnp.concatenate([keys] * (width // LANES), axis=1)
    return wide == tkey_ref[...]


def stats_kernel(
    pair_s, place_s, recv_ref, near_ref, far_ref, tkey_ref, cbt_ref,
    u_ref, q_ref, st_ref, codes_ref, unit_ref, inv_ref, rows_ref, key_ref,
):
    cols = u_ref.shape[0]
    pair_count = cols // PR
    rep = place_s[3]
    rows = near_ref.shape[0] // 2
    across = q_ref.shape[0] // rows - 1 - rep
    for owner, part in (
        (rep, near_ref[0:rows, :]),
        (rep ^ 1, near_ref[rows : 2 * rows, :]),
        (across, far_ref[0:rows, :]),
        (across ^ 1, far_ref[rows : 2 * rows, :]),
    ):
        q_ref[pl.ds(pl.multiple_of(owner * rows, rows), rows), :] = part
    rows_ref[...] = recv_ref[...].astype(F32)
    lane_group = lax.broadcasted_iota(jnp.int32, (BOOKS, LANES), 1) // PR
    per_tile = LANES // PR
    for tile in range(cols // LANES):
        held = jnp.zeros((BOOKS, LANES), F32)
        for place in range(per_tile):
            block = pair_s[0, tile * per_tile + place]
            owner = block >> 2
            within = block & 3
            codes = rows_ref[pl.ds(pl.multiple_of(owner * BOOKS, BOOKS), BOOKS), :]
            turned = pltpu.roll(codes, lax.rem(LANES + (place - within) * PR, LANES), axis=1)
            held = jnp.where(lane_group == place, turned, held)
        codes_ref[:, tile * LANES : (tile + 1) * LANES] = held
    fill_keys(pair_s, key_ref, pair_count)
    quant = jnp.zeros((cbt_ref.shape[0], cols), F32)
    for book in range(BOOKS):
        quant = quant + jnp.dot(
            cbt_ref[:, book * CODES : (book + 1) * CODES],
            one_hot_of(codes_ref, book, CODES),
            preferred_element_type=F32,
        )
    inverse = lax.rsqrt(jnp.sum(quant * quant, axis=0, keepdims=True) + EPS)
    unit = quant * inverse
    unit_ref[...] = unit
    inv_ref[...] = inverse
    u_ref[...] = unit.T.astype(BF16)
    total_rows = q_ref.shape[0]
    peak = jnp.full((1, total_rows), -1e30, F32)
    total = jnp.zeros((1, total_rows), F32)
    hit = jnp.zeros((1, total_rows), F32)
    step = min(256, cols)
    for start in range(0, cols, step):
        scores = lax.dot_general(
            u_ref[start : start + step, :], q_ref[...], CONTRACT_LAST, preferred_element_type=F32
        )
        fresh = jnp.maximum(peak, jnp.max(scores, axis=0, keepdims=True))
        total = total * jnp.exp(peak - fresh) + jnp.sum(
            jnp.exp(scores - fresh), axis=0, keepdims=True
        )
        peak = fresh
        hit = hit + jnp.sum(
            jnp.where(hits(key_ref, start, step, tkey_ref), scores, 0.0), axis=0, keepdims=True
        )
    st_ref[0:1, :] = peak
    st_ref[1:2, :] = total
    st_ref[2:3, :] = hit


def hot_kernel(codes_ref, u_ref, q_ref, st_ref, hot_ref, exp_ref):
    for book in range(BOOKS):
        hot_ref[book] = one_hot_of(codes_ref, book, CODES)
    cols = u_ref.shape[0]
    step = min(256, cols)
    for start in range(0, cols, step):
        span = slice(start, start + step)
        scores = lax.dot_general(
            u_ref[span, :], q_ref[...], CONTRACT_LAST, preferred_element_type=F32
        )
        exp_ref[span, :] = jnp.exp(scores - st_ref[0:1, :])


def pack_kernel(codes_hbm, pairs_hbm, out_ref, codes_ref, pairs_ref, sems):
    copies = [
        pltpu.make_async_copy(codes_hbm, codes_ref, sems.at[0]),
        pltpu.make_async_copy(pairs_hbm, pairs_ref, sems.at[1]),
    ]
    for copy in copies:
        copy.start()
    for copy in copies:
        copy.wait()
    codes = codes_ref[...]
    spare = LANES - codes.shape[1] - pairs_ref.shape[1]
    pieces = [codes, jnp.broadcast_to(pairs_ref[...], (BOOKS, pairs_ref.shape[1]))]
    if spare:
        pieces.append(jnp.zeros((BOOKS, spare), jnp.int32))
    message = jnp.concatenate(pieces, axis=1).astype(F32).astype(BF16)
    for peer in range(out_ref.shape[0]):
        out_ref[peer] = message


def side_kernel(
    place_s, codes_hbm, pairs_hbm, targets_hbm, books_hbm,
    pairs_ref, slot_ref, tkey_ref, cbt_ref, unit_ref,
    codes_ref, near_ref, targets_ref, books_ref, float_ref, sems,
):
    moves = (
        (codes_hbm, codes_ref),
        (pairs_hbm, near_ref),
        (targets_hbm, targets_ref),
        (books_hbm, books_ref),
    )
    copies = [pltpu.make_async_copy(a, b, sems.at[k]) for k, (a, b) in enumerate(moves)]
    for copy in copies:
        copy.start()
    for copy in copies:
        copy.wait()
    rep = place_s[3]
    pairs_ref[...] = near_ref[...]
    count = near_ref.shape[1]
    wide = jnp.broadcast_to(near_ref[...], (count, count))
    tall = wide.astype(F32).T.astype(jnp.int32)
    before = ((tall >> 2) == (wide >> 2)) & (tall < wide)
    slot_ref[...] = (near_ref[...] >> 2) * CAP + jnp.sum(
        jnp.where(before, 1, 0), axis=0, keepdims=True
    )
    reps, rows = targets_ref.shape
    for k in range(reps):
        target = targets_ref[k : k + 1, :]
        block = target // (PR * reps)
        within = target - block * (PR * reps)
        mine = within // PR == rep
        tkey_ref[:, k * rows : (k + 1) * rows] = jnp.where(
            mine, block * PR + within - rep * PR, -1
        )
    float_ref[...] = codes_ref[...].astype(F32)
    quant = jnp.zeros((unit_ref.shape[0], cbt_ref.shape[0]), F32)
    for book in range(BOOKS):
        span = slice(book * CODES, (book + 1) * CODES)
        words = books_ref[span, :]
        cbt_ref[:, span] = words.T
        quant = quant + lax.dot_general(
            one_hot_of(float_ref, book, CODES), words, CONTRACT_FIRST, preferred_element_type=F32
        )
    inverse = lax.rsqrt(jnp.sum(quant * quant, axis=1, keepdims=True) + EPS)
    feat = quant.shape[1]
    unit_ref[:, 0:feat] = quant * inverse
    unit_ref[:, feat:] = jnp.broadcast_to(inverse, (quant.shape[0], LANES))


def merged(first, second):
    peak = jnp.maximum(first[0:1], second[0:1])
    total = first[1:2] * jnp.exp(first[0:1] - peak) + second[1:2] * jnp.exp(second[0:1] - peak)
    return peak, total, first[2:3] + second[2:3]


def grads_kernel(
    pair_s, slot_s, place_s,
    st_ref, sta_ref, stb_ref, tkey_ref, u_ref, q_ref, unit_ref, inv_ref, hot_ref, exp_ref,
    send_ref, loss_ref, held_ref, lent_ref, stay_ref, give_ref,
    key_ref, lse_ref, qgt_ref, pg_ref, sum_ref, *, sizes,
):
    cols = u_ref.shape[0]
    pair_count = cols // PR
    x_here, z_here, rep = place_s[0], place_s[1], place_s[3]
    x_count, z_count = sizes
    rows = held_ref.shape[2]
    peak, total, hit = merged(sta_ref[...], stb_ref[...])
    lse = peak + jnp.log(total)
    factor = jnp.exp(st_ref[0:1, :] - lse)
    lse_ref[0:1, :] = lse - hit
    loss_ref[...] = lse_ref[0:1, pl.ds(pl.multiple_of(rep * rows, rows), rows)]
    fill_keys(pair_s, key_ref, pair_count)
    send_ref[...] = jnp.zeros(send_ref.shape, BF16)
    step = min(256, cols)
    grown = None
    for start in range(0, cols, step):
        span = slice(start, start + step)
        u_part = u_ref[span, :]
        hit_mask = hits(key_ref, start, step, tkey_ref)
        weight = (exp_ref[span, :] * factor - jnp.where(hit_mask, 1.0, 0.0)).astype(BF16)
        grad = jnp.dot(weight, q_ref[...], preferred_element_type=F32)
        narrow = grad.astype(BF16)
        for place in range(step // PR):
            send_ref[slot_s[0, start // PR + place]] = narrow[place * PR : (place + 1) * PR, :]
        turned = grad.T
        unit = unit_ref[:, span]
        along = jnp.sum(unit * turned, axis=0, keepdims=True)
        pg_ref[:, span] = (inv_ref[0:1, span] * (turned - unit * along)).astype(BF16)
        term = lax.dot_general(u_part, weight, CONTRACT_FIRST, preferred_element_type=F32)
        grown = term if grown is None else grown + term
    qgt_ref[...] = grown
    count = q_ref.shape[0] // rows
    for out, first in ((held_ref, rep), (lent_ref, rep ^ 1)):
        for k, owner in enumerate((first, count - 1 - first)):
            part = qgt_ref[:, pl.ds(pl.multiple_of(owner * rows, rows), rows)]
            out[k] = part.astype(out.dtype)
    for book in range(BOOKS):
        sum_ref[book * CODES : (book + 1) * CODES, :] = lax.dot_general(
            hot_ref[book], pg_ref[...], CONTRACT_LAST, preferred_element_type=F32
        )
    half = z_count // 2
    size = stay_ref.shape[1]
    z_order = halving_order(z_here, z_partners(z_count))
    for at, px in enumerate(halving_order(x_here, x_partners(x_count))):
        for k in range(half):
            near = pl.multiple_of((px * z_count + z_order[k]) * size, size)
            there = pl.multiple_of((px * z_count + z_order[half + k]) * size, size)
            stay_ref[at * half + k] = sum_ref[pl.ds(near, size), :]
            give_ref[at * half + k] = sum_ref[pl.ds(there, size), :].astype(BF16)


def x_partners(count):
    if count == 4:
        return [lambda i: i ^ 1, lambda i: 3 - i]
    return [lambda i: i ^ 1][: count - 1]


def z_partners(count):
    if count == 8:
        return [
            lambda i: i ^ 1,
            lambda i: (i - 1 + 2 * (i & 1)) & 7,
            lambda i: (i + 3 - 6 * (i & 1)) & 7,
        ]
    return [lambda i: i ^ 1][: count - 1]


def halving_order(here, partners):
    order = [here]
    for partner in reversed(partners):
        order = order + halving_tail(partner(here), partners, len(order))
    return order


def halving_tail(there, partners, length):
    order = [there]
    for partner in reversed(partners):
        if len(order) == length:
            break
        order = order + halving_tail(partner(there), partners, len(order))
    return order


def split_kernel(place_s, stay_ref, recv_ref, keep_ref, give_ref, sum_ref):
    core = place_s[2]
    half = keep_ref.shape[1]
    sum_ref[...] = stay_ref[...] + recv_ref[...].astype(F32)
    mine = pl.ds(pl.multiple_of(core * half, half), half)
    other = pl.ds(pl.multiple_of((1 - core) * half, half), half)
    for chunk in range(keep_ref.shape[0]):
        keep_ref[chunk] = sum_ref[chunk, mine, :]
        give_ref[chunk] = sum_ref[chunk, other, :].astype(BF16)


def deal_kernel(
    place_s, stay_ref, recv_ref, held_ref, back_ref,
    own_ref, far1, far2, far3, half_ref, over_ref, sum_ref,
):
    half_ref[...] = held_ref[0].astype(F32) + back_ref[0].astype(F32)
    over_ref[...] = (held_ref[1].astype(F32) + back_ref[1].astype(F32)).astype(BF16)
    rep = place_s[3]
    chunks = stay_ref.shape[0]
    share = own_ref.shape[0] // chunks
    reps = stay_ref.shape[1] // share
    sum_ref[...] = stay_ref[...] + recv_ref[...].astype(F32)
    for k, out in enumerate((own_ref, far1, far2, far3)):
        owner = lax.rem(rep + k, reps)
        at = pl.ds(pl.multiple_of(owner * share, share), share)
        for pair in range(chunks // 2):
            rows = jnp.concatenate(
                [sum_ref[2 * pair, at, :], sum_ref[2 * pair + 1, at, :]], axis=0
            )
            out[2 * pair * share : (2 * pair + 2) * share, :] = rows.astype(out.dtype)


def last_kernel(own_ref, far_ref, out_ref):
    out_ref[...] = (own_ref[...] + far_ref[...].astype(F32)).T


def return_kernel(slot_j, ret_ref, unit_ref, out_ref, *sums):
    for part in sums:
        part[...] = jnp.zeros(part.shape, F32)
    for slot in range(ret_ref.shape[0]):
        part = sums[slot % len(sums)]
        j = slot_j[slot]
        part[j] = part[j] + ret_ref[slot].astype(F32)
    for j in range(PBLK_DEV):
        grad = sums[0][j]
        for part in sums[1:]:
            grad = grad + part[j]
        feat = out_ref.shape[1]
        unit = unit_ref[j * PR : (j + 1) * PR, 0:feat]
        inverse = unit_ref[j * PR : (j + 1) * PR, feat : feat + 1]
        out_ref[j * PR : (j + 1) * PR, :] = inverse * (
            grad - unit * jnp.sum(unit * grad, axis=1, keepdims=True)
        )


def shifted(x, k):
    count = lax.axis_size("rep")
    return lax.ppermute(x, "rep", [(i, (i + k) % count) for i in range(count)])


def stepped(x, axis, partner):
    return lax.ppermute(x, axis, [(i, partner(i)) for i in range(lax.axis_size(axis))])


def shards(query_embed, positive_ids, pair_blocks, code_ids, codebooks):
    reps = lax.axis_size("rep")
    x_count, z_count, cores = (lax.axis_size(a) for a in BLK)
    owners = x_count * z_count * cores
    here_blk = lax.axis_index(BLK)
    rows_mine = query_embed[0, 0]
    row_count, feat = rows_mine.shape
    all_rows = reps * row_count
    wanted = pair_blocks[0]
    pair_count = wanted.shape[0]
    cols = pair_count * PR
    local_codes = code_ids[0, 0]
    place = jnp.stack([lax.axis_index(a) for a in AXES]).astype(jnp.int32)
    near = [(i, i ^ 1) for i in range(reps)]
    cross = [(i, reps - 1 - i) for i in range(reps)]
    pairs_in = wanted[None, :]
    held = local_codes.shape[1]

    rows_near = lax.ppermute(rows_mine, "rep", near)
    message = call(
        pack_kernel,
        sds((owners, BOOKS, LANES), BF16),
        [
            pltpu.VMEM((BOOKS, held), jnp.int32),
            pltpu.VMEM((1, pair_count), jnp.int32),
            pltpu.SemaphoreType.DMA((2,)),
        ],
        0,
        0,
        owners * BOOKS * LANES,
        2,
        WHOLE_VMEM,
    )(local_codes, pairs_in)
    arrived = lax.all_to_all(message, BLK, 0, 0, tiled=True)
    rows_pair = jnp.concatenate([rows_mine, rows_near], axis=0)
    rows_far = lax.ppermute(rows_pair, "rep", cross)
    pairs, slot_of, tkey, turned_books, unit = call(
        side_kernel,
        (
            sds((1, pair_count), jnp.int32),
            sds((1, pair_count), jnp.int32),
            sds((1, all_rows), jnp.int32),
            sds((feat, BOOKS * CODES), BF16),
            sds((held, feat + LANES), F32),
        ),
        [
            pltpu.VMEM((BOOKS, held), jnp.int32),
            pltpu.VMEM((1, pair_count), jnp.int32),
            pltpu.VMEM((reps, row_count), jnp.int32),
            pltpu.VMEM((BOOKS * CODES, feat), BF16),
            pltpu.VMEM((BOOKS, held), F32),
            pltpu.SemaphoreType.DMA((4,)),
        ],
        1,
        0,
        2 * BOOKS * CODES * feat * held,
        4,
    )(place, local_codes, pairs_in, positive_ids[0], codebooks)

    units, queries, stats, codes, unit_t, inv_t = call(
        stats_kernel,
        (
            sds((cols, feat), BF16),
            sds((all_rows, feat), BF16),
            sds((3, all_rows), F32),
            sds((BOOKS, cols), F32),
            sds((feat, cols), F32),
            sds((1, cols), F32),
        ),
        [pltpu.VMEM((owners * BOOKS, LANES), F32), pltpu.VMEM((cols, LANES), jnp.int32)],
        2,
        5,
        2 * cols * feat * (BOOKS * CODES + all_rows),
    )(
        pairs, place, arrived.reshape(owners * BOOKS, LANES),
        rows_pair, rows_far, tkey, turned_books,
    )

    stats_near = lax.ppermute(stats, "rep", near)
    hot, powers = call(
        hot_kernel,
        (sds((BOOKS, CODES, cols), BF16), sds((cols, all_rows), F32)),
        [],
        0,
        4,
        BOOKS * CODES * cols,
    )(codes, units, queries, stats)
    stats_two = jnp.concatenate(merged(stats, stats_near), axis=0)
    stats_far = lax.ppermute(stats_two, "rep", cross)

    chunks = x_count * z_count
    chunk_rows = codebooks.shape[0] // chunks
    half_rows = chunk_rows // cores
    held_chunks = chunks // 2
    outbound, loss, held_t, lent_t, stay, give = call(
        functools.partial(grads_kernel, sizes=(x_count, z_count)),
        (
            sds((owners * CAP, PR, feat), BF16),
            sds((1, row_count), F32),
            sds((2, feat, row_count), BF16),
            sds((2, feat, row_count), BF16),
            sds((held_chunks, chunk_rows, feat), F32),
            sds((held_chunks, chunk_rows, feat), BF16),
        ),
        [
            pltpu.VMEM((cols, LANES), jnp.int32),
            pltpu.VMEM((8, all_rows), F32),
            pltpu.VMEM((feat, all_rows), F32),
            pltpu.VMEM((feat, cols), BF16),
            pltpu.VMEM((BOOKS * CODES, feat), F32),
        ],
        3,
        10,
        cols * feat * (4 * all_rows + 2 * BOOKS * CODES),
    )(
        pairs, slot_of, place,
        stats, stats_two, stats_far, tkey, units, queries, unit_t, inv_t, hot, powers,
    )

    outbound = outbound.reshape(owners, CAP * PR, feat)
    returned = lax.all_to_all(outbound, BLK, 0, 0, tiled=True)
    returned = returned.reshape(owners * CAP, PR, feat)

    steps = [("z", partner) for partner in z_partners(z_count)]
    steps = steps[:1] + [("x", partner) for partner in x_partners(x_count)] + steps[1:]
    passed = stepped(give, *steps[0])
    lent_back = lax.ppermute(lent_t, "rep", near)
    keep, hand = call(
        split_kernel,
        (
            sds((held_chunks, half_rows, feat), F32),
            sds((held_chunks, half_rows, feat), BF16),
        ),
        [pltpu.VMEM((held_chunks, chunk_rows, feat), F32)],
        1,
        2,
        cols * feat,
    )(place, stay, passed)
    other = lax.ppermute(hand, "c", [(0, 1), (1, 0)])
    share_rows = half_rows // reps
    dealt = held_chunks * share_rows
    mine, *parts, own_t, far_t = call(
        deal_kernel,
        (
            sds((dealt, feat), F32),
            *[sds((dealt, feat), BF16)] * 3,
            sds((feat, row_count), F32),
            sds((feat, row_count), BF16),
        ),
        [pltpu.VMEM((held_chunks, half_rows, feat), F32)],
        1,
        4,
        cols * feat,
    )(place, keep, other, held_t, lent_back)
    far_t = lax.ppermute(far_t, "rep", cross)
    parts = [shifted(part, k + 1) for k, part in enumerate(parts)]
    for part in parts:
        mine = mine + part.astype(F32)
    query_grad = call(
        last_kernel, sds((row_count, feat), F32), [], 0, 2, row_count * feat
    )(own_t, far_t)
    for axis, partner in steps[1:]:
        half = mine.shape[0] // 2
        more = stepped(mine[half:].astype(BF16), axis, partner)
        mine = mine[:half] + more.astype(F32)
    codebook_grad = mine

    directory = arrived[:, 0, held : held + pair_count].astype(jnp.int32)
    local_iota = jnp.arange(PBLK_DEV, dtype=jnp.int32)
    named = jnp.any(
        directory[:, :, None] == here_blk * PBLK_DEV + local_iota[None, None, :], axis=1
    )
    slot_j = []
    for k in range(CAP):
        rank = jnp.zeros((owners,), jnp.int32)
        found = jnp.full((owners,), PBLK_DEV, jnp.int32)
        for j in range(PBLK_DEV):
            found = jnp.where(named[:, j] & (rank == k), j, found)
            rank = rank + named[:, j].astype(jnp.int32)
        slot_j.append(found)
    slot_j = jnp.stack(slot_j, axis=1).reshape(-1)
    passage_grad = call(
        return_kernel,
        sds((PBLK_DEV * PR, feat), F32),
        [pltpu.VMEM((PBLK_DEV + 1, PR, feat), F32) for _ in range(4)],
        1,
        2,
        owners * CAP * PR * feat,
    )(slot_j, returned, unit)
    return (
        loss[None],
        query_grad[None, None],
        passage_grad[None, None],
        codebook_grad,
    )


def solution(mesh):
    reps = mesh.shape["rep"]
    torus = Mesh(mesh.devices.reshape(4, -1, 2, reps), AXES)
    in_specs = (
        P(BLK, "rep", None, None),
        P(BLK, None, None),
        P(BLK, None),
        P(BLK, "rep", None, None),
        P(),
    )
    out_specs = (
        P(BLK, "rep", None),
        P(BLK, "rep", None, None),
        P(BLK, "rep", None, None),
        P(AXES, None),
    )
    return jax.shard_map(
        shards, mesh=torus, in_specs=in_specs, out_specs=out_specs, check_vma=False
    )
```
